128 devices in a mesh: layer: 4 (over y), latent: 16 (over x, z), tok: 2 (over core).
Axes of the slice: x: 4, y: 4, z: 4, core: 2. Of those that a mesh axis runs over, the one named last changes fastest.
Arguments:
- resid_in: bfloat16 [4, 1024, 2304], P('layer', 'tok'), may hold values from -6 to 6
- resid_out: bfloat16 [4, 1024, 2304], P('layer', 'tok', 'latent'), may hold values from -6 to 6
- enc_weight: bfloat16 [4, 2304, 8192], P('layer', None, 'latent'), may hold values from -0.125 to 0.125
- enc_bias: float32 [4, 8192], P('layer', 'latent'), may hold values from -1 to 1
- dec_weight: bfloat16 [4, 4, 8192, 2304], P('layer', None, 'latent'), may hold values from -0.09375 to 0.09375
- dec_bias: float32 [4, 2304], P('layer', 'latent'), may hold values from -3 to 3
Outputs:
- dec_grad: float32 [4, 4, 8192, 2304], P('layer', None, 'latent', 'tok')
- dec_bias_grad: float32 [4, 2304], P('layer', 'latent')
- enc_grad: float32 [4, 2304, 8192], P('layer', 'tok', 'latent')
- enc_bias_grad: float32 [4, 8192], P('layer', 'latent')
The draws below stay inside these ranges and needn't reach their ends.
All inputs are finite; a program needn't handle non-finite values.
Results may differ from the reference program's by a relative error of at most 0.0045.
Values may be sent and summed in bfloat16 or wider, within the bound.
No kernel may reach another device: no remote copies, remote signals or barrier semaphores. Data moves between devices by JAX's collectives and lax.ppermute only.
A program may use at most 128 MiB of HBM per device.

```python
import math
import jax
import jax.numpy as jnp
from jax import lax

D = 2304
F = 8192
LAYERS = 4
TOKENS = 1024


def spiked(entries, rng, source, target, parts, factor):
    owner, partner = [(jnp.arange(entries.shape[dim]) // (entries.shape[dim] // parts)).reshape([-1 if axis == dim else 1 for axis in range(entries.ndim)]) for dim in (source, target)]
    chosen = jax.random.permutation(rng, parts)[partner]
    strong = (owner == chosen) | (owner == (partner + parts // 2) % parts)
    return jnp.where(strong, factor * entries, entries)


def steps_of(stream_key, extent, split, least, high):
    level = 1.0
    for position, shards_of in split:
        heights = jax.random.uniform(jax.random.fold_in(jax.random.fold_in(stream_key, 6), position), (shards_of,), jnp.float32, least / len(split), high / len(split))
        level = level * jnp.repeat(jnp.exp(heights), extent[position] // shards_of).reshape((-1,) + (1,) * (len(extent) - 1 - position))
    return level


def noise(key, extent, scale, limit, shards=(), kind=jnp.bfloat16):
    entries = scale * jax.random.normal(key, extent, jnp.float32)
    if shards:
        entries = entries * steps_of(key, extent, shards, -0.22, 0.18)
    return jnp.clip(entries, -limit, limit).astype(kind)


def noise_with(rng, extent, width, reach, shards, heavy, dtype=jnp.bfloat16):
    values = width * jax.random.normal(rng, extent, jnp.float32)
    if shards:
        values = values * steps_of(rng, extent, shards, -0.22, 0.18)
    return jnp.clip(spiked(values, jax.random.fold_in(rng, 3), *heavy), -reach, reach).astype(dtype)


def setup_inputs(seed: int = 0) -> dict:
    key_list = jax.random.split(jax.random.key(seed), 7)
    return {
        "resid_in": noise(key_list[0], (LAYERS, TOKENS, D), 1.0, 6.0, ((0, 4), (1, 2))),
        "resid_out": noise(key_list[1], (LAYERS, TOKENS, D), 1.0, 6.0, ((0, 4), (1, 2), (2, 16))),
        "enc_weight": noise(key_list[2], (LAYERS, D, F), D ** -0.5, 0.125, ((0, 4), (2, 16))),
        "enc_bias": jnp.clip(jax.random.uniform(key_list[3], (LAYERS, F), jnp.float32, -1.0, 1.0) * steps_of(key_list[3], (LAYERS, F), ((0, 4), (1, 16)), -0.4, 0.0), -1.0, 1.0),
        "dec_weight": noise_with(key_list[4], (LAYERS, LAYERS, F, D), F ** -0.5, 0.09375, ((0, 4), (2, 16)), (2, 3, 16, 2.0)),
        "dec_bias": noise(key_list[5], (LAYERS, D), 0.5, 3.0, ((0, 4), (1, 16)), jnp.float32),
    }


def smooth(values):
    return jax.nn.gelu(values, approximate=True)

def reference(resid_in, resid_out, enc_weight, enc_bias, dec_weight, dec_bias):
    loss_scale = 1.0 / math.sqrt(TOKENS)
    pre_list = []
    latent_list = []
    for src_layer in range(LAYERS):
        pre_act = jnp.dot(resid_in[src_layer], enc_weight[src_layer], preferred_element_type=jnp.float32) + enc_bias[src_layer]
        pre_list.append(pre_act)
        latent_list.append(smooth(pre_act).astype(jnp.bfloat16))
    error_list = []
    dec_bias_rows = []
    for dst_layer in range(LAYERS):
        summed = jnp.zeros((TOKENS, D), jnp.float32)
        for src_layer in range(dst_layer + 1):
            summed = summed + jnp.dot(latent_list[src_layer], dec_weight[src_layer, dst_layer], preferred_element_type=jnp.float32)
        errors = ((summed + dec_bias[dst_layer] - resid_out[dst_layer].astype(jnp.float32)) * loss_scale).astype(jnp.bfloat16)
        error_list.append(errors)
        dec_bias_rows.append(lax.optimization_barrier(jnp.sum(errors.astype(jnp.float32), axis=0)))
    dec_rows = []
    enc_rows = []
    enc_bias_rows = []
    for src_layer in range(LAYERS):
        blocks = []
        act_grad = jnp.zeros((TOKENS, F), jnp.float32)
        for dst_layer in range(LAYERS):
            if dst_layer >= src_layer:
                blocks.append(jnp.dot(latent_list[src_layer].T, error_list[dst_layer], preferred_element_type=jnp.float32))
                act_grad = act_grad + jnp.dot(error_list[dst_layer], dec_weight[src_layer, dst_layer].T, preferred_element_type=jnp.float32)
            else:
                blocks.append(jnp.zeros((F, D), jnp.float32))
        dec_rows.append(jnp.stack(blocks))
        pre_grad = jax.vjp(smooth, pre_list[src_layer])[1](act_grad)[0].astype(jnp.bfloat16)
        enc_rows.append(jnp.dot(resid_in[src_layer].T, pre_grad, preferred_element_type=jnp.float32))
        enc_bias_rows.append(lax.optimization_barrier(jnp.sum(pre_grad.astype(jnp.float32), axis=0)))
    return (jnp.stack(dec_rows), jnp.stack(dec_bias_rows), jnp.stack(enc_rows), jnp.stack(enc_bias_rows))
```

```python
import functools
import math

import jax
import jax.numpy as jnp
from jax import lax
from jax.experimental import pallas as pl
from jax.experimental.pallas import tpu as pltpu
from jax.sharding import PartitionSpec as P

LAYER, LX, LZ, TOK = "layer", "lx", "lz", "tok"
BF16, F32 = jnp.bfloat16, jnp.float32


def smooth(values):
    return jax.nn.gelu(values, approximate=True)


def shift(value, axis, step):
    n = lax.axis_size(axis)
    return lax.ppermute(value, axis, [(i, (i + step) % n) for i in range(n)])


def send_up(value, step):
    n = lax.axis_size(LAYER)
    pairs = [(i, i + step) for i in range(n) if 0 <= i + step < n]
    return lax.ppermute(value, LAYER, pairs)


def swap(value):
    return lax.ppermute(value, TOK, [(0, 1), (1, 0)])


def turned(value, axis, by):
    n = value.shape[axis]
    return lax.dynamic_slice_in_dim(jnp.concatenate([value, value], axis), by, n, axis)


def spread(value, axis):
    return [value[0]] + [shift(value[k], axis, k) for k in range(1, len(value))]


def gathered(value, axis):
    n = lax.axis_size(axis)
    return [value] + [shift(value, axis, -k) for k in range(1, n)]


def total(values):
    return functools.reduce(jnp.add, [v.astype(F32) for v in values])


def params():
    return pltpu.CompilerParams(vmem_limit_bytes=56 * 2**20)


def y_kernel(where, lat_ref, w_ref, y_ref, *, cols):
    live = where[0] + pl.program_id(0) < pl.num_programs(0)

    @pl.when(live)
    def _():
        y_ref[0] = jnp.dot(
            lat_ref[...], w_ref[0, :, :cols], preferred_element_type=F32
        ).astype(BF16)

    @pl.when(jnp.logical_not(live))
    def _():
        y_ref[0] = jnp.zeros_like(y_ref[0])


def x_kernel(where, lat_ref, w_ref, *out_refs, cols):
    rows = out_refs[0].shape[1]
    for i, out in enumerate(out_refs):
        out[0] = jnp.dot(
            lat_ref[i * rows : (i + 1) * rows, :],
            w_ref[0, :, cols:],
            preferred_element_type=F32,
        ).astype(BF16)


def rebuild_y(where, lat, weights, width, cols):
    layers, feats, _ = weights.shape
    rows = lat.shape[0]
    return pl.pallas_call(
        functools.partial(y_kernel, cols=cols),
        out_shape=jax.ShapeDtypeStruct((layers, rows, cols), BF16),
        grid_spec=pltpu.PrefetchScalarGridSpec(
            num_scalar_prefetch=1,
            grid=(layers,),
            in_specs=[
                pl.BlockSpec((rows, feats), lambda k, w: (0, 0)),
                pl.BlockSpec((1, feats, width), lambda k, w: (lax.rem(w[0] + k, layers), 0, w[1])),
            ],
            out_specs=pl.BlockSpec((1, rows, cols), lambda k, w: (lax.rem(w[0] + k, layers), 0, 0)),
        ),
        compiler_params=params(),
        cost_estimate=pl.CostEstimate(
            flops=2 * layers * rows * feats * cols, bytes_accessed=10 * 2**20, transcendentals=0
        ),
    )(where, lat, weights)


def rebuild_x(where, lat, weights, width, cols, first, count, parts):
    layers, feats, _ = weights.shape
    rows = lat.shape[0]
    step = rows // parts
    return pl.pallas_call(
        functools.partial(x_kernel, cols=cols),
        out_shape=[jax.ShapeDtypeStruct((count, step, width - cols), BF16)] * parts,
        grid_spec=pltpu.PrefetchScalarGridSpec(
            num_scalar_prefetch=1,
            grid=(count,),
            in_specs=[
                pl.BlockSpec((rows, feats), lambda k, w: (0, 0)),
                pl.BlockSpec(
                    (1, feats, width), lambda k, w: (lax.rem(w[0] + first + k, layers), 0, w[1])
                ),
            ],
            out_specs=[pl.BlockSpec((1, step, width - cols), lambda k, w: (k, 0, 0))] * parts,
        ),
        compiler_params=params(),
        cost_estimate=pl.CostEstimate(
            flops=2 * count * rows * feats * (width - cols),
            bytes_accessed=8 * 2**20,
            transcendentals=0,
        ),
    )(where, lat, weights)


def grad_kernel(where, lat_t_ref, w_ref, y_ref, *refs, parts, cols, ring):
    x_refs = refs[:parts]
    dec_ref, own_ref, other_ref, sum_ref, err_ref, act_ref = refs[parts:]
    k = pl.program_id(0)
    live = where[0] + k < pl.num_programs(0)
    rows = err_ref.shape[0]
    step = rows // parts

    @pl.when(live)
    def _():
        err_ref[:, :cols] = y_ref[0]
        for i, x_ref in enumerate(x_refs):
            err_ref[i * step : (i + 1) * step, cols:] = x_ref[0]
        half = lat_t_ref.shape[0] // 2
        for i in range(2):
            dec_ref[0, i * half : (i + 1) * half, :] = jnp.dot(
                lat_t_ref[i * half : (i + 1) * half, :], err_ref[...], preferred_element_type=F32
            )
        for i in range(2):
            add = lax.dot_general(
                err_ref[...],
                w_ref[0, i * half : (i + 1) * half, :],
                (((1,), (1,)), ((), ())),
                preferred_element_type=F32,
            )
            here = slice(i * half, (i + 1) * half)

            @pl.when(k == 0)
            def _():
                act_ref[:, here] = add

            @pl.when(k > 0)
            def _():
                act_ref[:, here] += add

    @pl.when(jnp.logical_not(live))
    def _():
        dec_ref[0] = jnp.zeros_like(dec_ref[0])

    @pl.when(k == 0)
    def _():
        sum_ref[...] = jnp.sum(err_ref[...].astype(F32), axis=0, keepdims=True)

    @pl.when(k == pl.num_programs(0) - 1)
    def _():
        own_ref[...] = act_ref[: rows // 2, :]
        piece = rows // 2 // ring // ring
        for i in range(ring):
            for j in range(ring):
                to, at = (i * ring + j) * piece, rows // 2 + (j * ring + i) * piece
                other_ref[to : to + piece, :] = act_ref[at : at + piece, :]


def grads(where, lat_t, weights, err_y, err_x, width, ring):
    layers, feats, _ = weights.shape
    rows = lat_t.shape[1]
    cols, parts = err_y.shape[2], len(err_x)
    return pl.pallas_call(
        functools.partial(grad_kernel, parts=parts, cols=cols, ring=ring),
        out_shape=[
            jax.ShapeDtypeStruct((layers, feats, width), F32),
            jax.ShapeDtypeStruct((rows // 2, feats), F32),
            jax.ShapeDtypeStruct((rows // 2, feats), F32),
            jax.ShapeDtypeStruct((1, width), F32),
        ],
        grid_spec=pltpu.PrefetchScalarGridSpec(
            num_scalar_prefetch=1,
            grid=(layers,),
            in_specs=[
                pl.BlockSpec((feats, rows), lambda k, w: (0, 0)),
                pl.BlockSpec((1, feats, width), lambda k, w: (lax.rem(w[0] + k, layers), 0, w[1])),
                pl.BlockSpec((1, rows, cols), lambda k, w: (lax.rem(w[0] + k, layers), 0, 0)),
            ]
            + [pl.BlockSpec((1, rows // parts, width - cols), lambda k, w: (k, 0, 0))] * parts,
            out_specs=[
                pl.BlockSpec((1, feats, width), lambda k, w: (lax.rem(w[0] + k, layers), 0, 0)),
                pl.BlockSpec((rows // 2, feats), lambda k, w: (0, 0)),
                pl.BlockSpec((rows // 2, feats), lambda k, w: (0, 0)),
                pl.BlockSpec((1, width), lambda k, w: (0, 0)),
            ],
            scratch_shapes=[pltpu.VMEM((rows, width), BF16), pltpu.VMEM((rows, feats), F32)],
        ),
        compiler_params=params(),
        cost_estimate=pl.CostEstimate(
            flops=4 * layers * rows * feats * width, bytes_accessed=40 * 2**20, transcendentals=0
        ),
    )(where, lat_t, weights, err_y, *err_x)


def on_device(resid_in, resid_out, enc_weight, enc_bias, dec_weight, dec_bias):
    s, x, z, c = (lax.axis_index(a) for a in (LAYER, LX, LZ, TOK))
    ring = lax.axis_size(LX)
    layers, feats, model = dec_weight.shape[1:]
    tok = resid_in.shape[1]
    width = model // 2
    cols = width // 3
    piece = tok // (ring * ring)
    scale = 1.0 / math.sqrt(tok * lax.axis_size(TOK))
    where = jnp.stack([s, c]).astype(jnp.int32)
    inputs, weights = resid_in[0], dec_weight[0]

    def mine_first(rows):
        blocks = rows.reshape(ring, ring, piece, rows.shape[1])
        return turned(turned(blocks, 0, x), 1, z).reshape(rows.shape)

    def crossed(rows):
        blocks = rows.reshape(ring, ring, -1, rows.shape[1])
        return blocks.transpose(1, 0, 2, 3).reshape(rows.shape)

    pre = mine_first(jnp.dot(inputs, enc_weight[0], preferred_element_type=F32) + enc_bias[0])
    own_lat = smooth(pre).astype(BF16)
    lat = jnp.concatenate([own_lat, crossed(swap(own_lat))], 0)

    y_part = rebuild_y(where, lat, weights, width, cols)
    y_sum = lax.psum_scatter(y_part, LAYER, scatter_dimension=0, tiled=True)[0]

    got_a, got_b = [], []
    for first in (0, 2):
        out = rebuild_x(where, lat, weights, width, cols, first, 2, 2 * ring)
        a, b = spread(out[:ring], LX), spread(out[ring:], LZ)
        got_a.append(total(a))
        got_b.append(total(b))
    lat, own_lat, anchor = lax.optimization_barrier((lat, own_lat, resid_out))
    lat_t = lat.T
    x_a, x_b = (jnp.concatenate(g, 0).astype(BF16) for g in (got_a, got_b))

    own_base = anchor[0].reshape(ring * ring, piece, -1)
    base = jnp.stack([own_base, swap(own_base)]).astype(F32)
    base = lax.all_to_all(dec_bias[0] - base, (LX, LZ), 1, 1, tiled=True)
    base = lax.dynamic_slice_in_dim(base, c * (ring * ring // 2), ring * ring // 2, 1)
    base = base.transpose(0, 2, 1, 3).reshape(2, piece, width)

    def second(a, b):
        a, b = (v.reshape(*v.shape[:-2], ring, piece, v.shape[-1]) for v in (a, b))
        a = total(spread([a[..., i, :, :] for i in range(ring)], LZ))
        b = total(spread([b[..., i, :, :] for i in range(ring)], LX))
        return jnp.stack([a, b])

    x_part = second(x_a, x_b)
    x_sum = x_part[:, 0]
    for k in range(1, layers):
        x_sum = x_sum + send_up(x_part[:, k].astype(BF16), k).astype(F32)

    y_a, y_b = (v.reshape(ring, ring * piece, cols) for v in (y_sum[:tok], y_sum[tok:]))
    y_a, y_b = (total(spread(list(v), d)).astype(BF16) for v, d in ((y_a, LX), (y_b, LZ)))
    rebuilt = jnp.concatenate([second(y_a, y_b), x_sum], 2)
    errors = ((rebuilt + base) * scale).astype(BF16)

    y_err, x_err = errors[..., :cols], errors[..., cols:]
    a = jnp.concatenate(gathered(jnp.concatenate(gathered(y_err[0], LZ), 0), LX), 0)
    b = jnp.concatenate(gathered(jnp.concatenate(gathered(y_err[1], LX), 0), LZ), 0)
    err_y = lax.all_gather(jnp.concatenate([a, b], 0)[None], LAYER, axis=0, tiled=True)
    x_all = jnp.stack([x_err] + [send_up(x_err, -k) for k in range(1, layers)], 1)
    a = gathered(jnp.concatenate(gathered(x_all[0], LZ), 1), LX)
    b = gathered(jnp.concatenate(gathered(x_all[1], LX), 1), LZ)

    dec_grad, own_act, other_act, sums = grads(where, lat_t, weights, err_y, a + b, width, ring)
    act = own_act + swap(other_act)
    pre_grad = jax.vjp(smooth, pre)[1](act)[0].astype(BF16)

    ordered = mine_first(inputs)
    own_in = lax.dynamic_slice_in_dim(ordered, c * width, width, 1)
    other_in = swap(lax.dynamic_slice_in_dim(ordered, (1 - c) * width, width, 1))
    both_in = jnp.concatenate([own_in, other_in], 0)
    both_grad = jnp.concatenate([pre_grad, swap(pre_grad)], 0)
    enc_grad = lax.dot_general(
        both_in, both_grad, (((0,), (0,)), ((), ())), preferred_element_type=F32
    )
    own_sum = jnp.sum(pre_grad.astype(F32), axis=0, keepdims=True)
    enc_bias_grad = own_sum + swap(own_sum)
    both = turned(jnp.concatenate([sums, swap(sums)], 0), 0, c).reshape(1, model)
    size = dec_bias.shape[1]
    dec_bias_grad = lax.dynamic_slice_in_dim(both, (x * ring + z) * size, size, 1)
    return dec_grad[None], dec_bias_grad, enc_grad[None], enc_bias_grad


def solution(mesh):
    ring = math.isqrt(mesh.shape["latent"])
    shape = (mesh.shape["layer"], ring, ring, mesh.shape["tok"])
    fine = jax.sharding.Mesh(mesh.devices.reshape(shape), (LAYER, LX, LZ, TOK))
    latent = (LX, LZ)
    in_specs = (
        P(LAYER, TOK, None),
        P(LAYER, TOK, latent),
        P(LAYER, None, latent),
        P(LAYER, latent),
        P(LAYER, None, latent, None),
        P(LAYER, latent),
    )
    out_specs = (
        P(LAYER, None, latent, TOK),
        P(LAYER, latent),
        P(LAYER, TOK, latent),
        P(LAYER, latent),
    )
    return jax.shard_map(
        on_device, mesh=fine, in_specs=in_specs, out_specs=out_specs, check_vma=False
    )
```

```python
import functools
import math

import jax
import jax.numpy as jnp
from jax import lax
from jax.experimental import pallas as pl
from jax.experimental.pallas import tpu as pltpu
from jax.sharding import PartitionSpec as P

LAYER, LX, LZ, TOK = "layer", "lx", "lz", "tok"
BF16, F32 = jnp.bfloat16, jnp.float32


def smooth(values):
    return jax.nn.gelu(values, approximate=True)


def shift(value, axis, step):
    n = lax.axis_size(axis)
    return lax.ppermute(value, axis, [(i, (i + step) % n) for i in range(n)])


def send_up(value, step):
    n = lax.axis_size(LAYER)
    pairs = [(i, i + step) for i in range(n) if 0 <= i + step < n]
    return lax.ppermute(value, LAYER, pairs)


def swap(value):
    return lax.ppermute(value, TOK, [(0, 1), (1, 0)])


def turned(value, axis, by):
    n = value.shape[axis]
    return lax.dynamic_slice_in_dim(jnp.concatenate([value, value], axis), by, n, axis)


def total(values):
    return functools.reduce(jnp.add, [v.astype(F32) for v in values])


def spread(value, axis):
    return [value[0]] + [shift(value[k], axis, k) for k in range(1, len(value))]


def gathered(value, axis):
    n = lax.axis_size(axis)
    return [value] + [shift(value, axis, -k) for k in range(1, n)]


def ring_spread(own, up, down, far_up, far_down, axis):
    half = far_up.shape[1]
    from_below, from_above = shift(far_up, axis, 1), shift(far_down, axis, -1)
    up = jnp.concatenate([total([up[:, :half], from_below]).astype(BF16), up[:, half:]], 1)
    down = jnp.concatenate([down[:, :half], total([down[:, half:], from_above]).astype(BF16)], 1)
    return total([own, shift(up, axis, 1), shift(down, axis, -1)])


def ring_gather(value, axis):
    half = value.shape[1] // 2
    above, below = shift(value, axis, -1), shift(value, axis, 1)
    return [value, above, below], [
        shift(above[:, :half], axis, -1),
        shift(below[:, half:], axis, 1),
    ]


def call(kernel, where, inputs, in_specs, outs, out_specs, grid, scratch, flops, moved, aliases=None):
    return pl.pallas_call(
        kernel,
        out_shape=[jax.ShapeDtypeStruct(shape, dtype) for shape, dtype in outs],
        grid_spec=pltpu.PrefetchScalarGridSpec(
            num_scalar_prefetch=1,
            grid=(grid,),
            in_specs=in_specs,
            out_specs=out_specs,
            scratch_shapes=scratch,
        ),
        input_output_aliases=aliases or {},
        compiler_params=pltpu.CompilerParams(vmem_limit_bytes=56 * 2**20),
        cost_estimate=pl.CostEstimate(flops=flops, bytes_accessed=moved, transcendentals=0),
    )(where, *inputs)


def fixed(*shape):
    return pl.BlockSpec(shape, lambda k, w: (0,) * len(shape))


def each(*shape):
    return pl.BlockSpec(shape, lambda k, w: (k,) + (0,) * (len(shape) - 1))


def encode_kernel(where, in_ref, w_ref, bias_ref, pre_ref, lat_ref, acc_ref, *, ring):
    k = pl.program_id(0)

    @pl.when(k == 0)
    def _():
        acc_ref[...] = jnp.broadcast_to(bias_ref[...], acc_ref.shape)

    acc_ref[...] += jnp.dot(in_ref[...], w_ref[...], preferred_element_type=F32)

    @pl.when(k == pl.num_programs(0) - 1)
    def _():
        piece = acc_ref.shape[0] // (ring * ring)
        for i in range(ring):
            for j in range(ring):
                row = lax.rem(i + ring - where[2], ring) * ring + lax.rem(j + ring - where[3], ring)
                pre = acc_ref[(i * ring + j) * piece : (i * ring + j + 1) * piece, :]
                to = pl.ds(pl.multiple_of(row * piece, piece), piece)
                pre_ref[to, :] = pre
                lat_ref[to, :] = smooth(pre).astype(BF16)


def encode(where, inputs, weight, bias, ring, steps=3):
    rows, model = inputs.shape
    feats = weight.shape[1]
    return call(
        functools.partial(encode_kernel, ring=ring),
        where,
        (inputs, weight, bias),
        [
            pl.BlockSpec((rows, model // steps), lambda k, w: (0, k)),
            pl.BlockSpec((model // steps, feats), lambda k, w: (k, 0)),
            fixed(1, feats),
        ],
        [((rows, feats), F32), ((rows, feats), BF16)],
        [fixed(rows, feats), fixed(rows, feats)],
        steps,
        [pltpu.VMEM((rows, feats), F32)],
        2 * rows * model * feats,
        8 * 2**20,
    )


def rebuild_kernel(where, lat_ref, w_ref, own_ref, up_ref, down_ref, far_up_ref, far_down_ref):
    out = jnp.dot(lat_ref[...], w_ref[0], preferred_element_type=F32)
    n = own_ref.shape[1]
    own_ref[0] = out[:n]
    out = out.astype(BF16)
    up_ref[0] = out[n : 2 * n]
    far_up_ref[0] = out[2 * n : 2 * n + n // 2]
    far_down_ref[0] = out[2 * n + n // 2 : 3 * n]
    down_ref[0] = out[3 * n :]


def rebuild(where, lat, weights, width):
    layers, feats, _ = weights.shape
    rows = lat.shape[0]
    n = rows // 4
    return call(
        rebuild_kernel,
        where,
        (lat, weights),
        [
            fixed(rows, feats),
            pl.BlockSpec((1, feats, width), lambda k, w: (lax.rem(w[0] + k, layers), 0, w[1])),
        ],
        [((layers, n, width), F32)]
        + [((layers, n, width), BF16)] * 2
        + [((layers, n // 2, width), BF16)] * 2,
        [each(1, n, width)] * 3 + [each(1, n // 2, width)] * 2,
        layers,
        [],
        2 * layers * rows * feats * width,
        12 * 2**20,
    )


def near_kernel(where, lat_ref, w_ref, *refs):
    *x_refs, dec_ref, act_ref, sum_ref, err_ref = refs
    k = pl.program_id(0)
    live = where[0] + k < pl.num_programs(0)
    step = x_refs[0].shape[1]

    @pl.when(k == 0)
    def _():
        act_ref[...] = jnp.zeros_like(act_ref)

    @pl.when(live)
    def _():
        for i, x_ref in enumerate(x_refs):
            err_ref[i * step : (i + 1) * step, :] = x_ref[0]
        dec_ref[0] = lax.dot_general(
            lat_ref[...], err_ref[...], (((0,), (0,)), ((), ())), preferred_element_type=F32
        )
        for i in range(0, err_ref.shape[0], 256):
            act_ref[i : i + 256, :] += lax.dot_general(
                err_ref[i : i + 256, :], w_ref[0], (((1,), (1,)), ((), ())), preferred_element_type=F32
            )

    @pl.when(jnp.logical_not(live))
    def _():
        dec_ref[0] = jnp.zeros_like(dec_ref[0])

    @pl.when(k == 0)
    def _():
        sum_ref[...] = jnp.sum(err_ref[...].astype(F32), axis=0, keepdims=True)


def far_kernel(where, lat_ref, w_ref, last_dec_ref, last_act_ref, last_sum_ref, *refs, ring):
    *x_refs, dec_ref, own_ref, other_ref, sum_ref, err_ref, act_ref = refs
    k = pl.program_id(0)
    live = where[0] + k < pl.num_programs(0)
    step = x_refs[0].shape[1]

    @pl.when(k == 0)
    def _():
        act_ref[...] = jnp.zeros_like(act_ref)

    @pl.when(live)
    def _():
        for i, x_ref in enumerate(x_refs):
            err_ref[i * step : (i + 1) * step, :] = x_ref[0]
        dec_ref[0] = last_dec_ref[0] + lax.dot_general(
            lat_ref[...], err_ref[...], (((0,), (0,)), ((), ())), preferred_element_type=F32
        )
        act_ref[...] += lax.dot_general(
            err_ref[...], w_ref[0], (((1,), (1,)), ((), ())), preferred_element_type=F32
        )

    @pl.when(jnp.logical_not(live))
    def _():
        dec_ref[0] = jnp.zeros_like(dec_ref[0])

    @pl.when(k == 0)
    def _():
        sum_ref[...] = last_sum_ref[...] + jnp.sum(err_ref[...].astype(F32), axis=0, keepdims=True)

    @pl.when(k == pl.num_programs(0) - 1)
    def _():
        n = act_ref.shape[0] // 2
        piece = n // ring
        for side in range(2):
            for i in range(ring):
                ref, at = {
                    0: (last_act_ref, 3 * n * side),
                    1: (last_act_ref, 3 * n * side + n),
                    2: (act_ref, n * side),
                    3: (last_act_ref, 3 * n * side + 2 * n),
                }[i]
                if side == 0:
                    own_ref[i * n : (i + 1) * n, :] = ref[at : at + n, :]
                else:
                    for j in range(ring):
                        to = (j * ring + i) * piece
                        other_ref[to : to + piece, :] = ref[at + j * piece : at + (j + 1) * piece, :]


def grads(where, lat, weights, near, far, width, ring):
    layers, feats, _ = weights.shape
    n = near[0].shape[1]
    blocks = [lat[i * n : (i + 1) * n] for i in range(2 * ring)]
    first = jnp.concatenate([blocks[i] for i in (0, 1, 3, 4, 5, 7)], 0)
    second = jnp.concatenate([blocks[2], blocks[6]], 0)
    target = pl.BlockSpec((1, feats, width), lambda k, w: (lax.rem(w[0] + k, layers), 0, w[1]))
    placed = pl.BlockSpec((1, feats, width), lambda k, w: (lax.rem(w[0] + k, layers), 0, 0))
    dec, act, sums = call(
        near_kernel,
        where,
        (first, weights, *near),
        [fixed(6 * n, feats), target] + [each(1, n, width)] * 6,
        [((layers, feats, width), F32), ((6 * n, feats), F32), ((1, width), F32)],
        [placed, fixed(6 * n, feats), fixed(1, width)],
        layers,
        [pltpu.VMEM((6 * n, width), BF16)],
        4 * layers * 6 * n * feats * width,
        25 * 2**20,
    )
    return call(
        functools.partial(far_kernel, ring=ring),
        where,
        (second, weights, dec, act, sums, *far),
        [fixed(2 * n, feats), target, placed, fixed(6 * n, feats), fixed(1, width)]
        + [each(1, n // 2, width)] * 4,
        [((layers, feats, width), F32)] + [((4 * n, feats), F32)] * 2 + [((1, width), F32)],
        [placed, fixed(4 * n, feats), fixed(4 * n, feats), fixed(1, width)],
        layers,
        [pltpu.VMEM((2 * n, width), BF16), pltpu.VMEM((2 * n, feats), F32)],
        4 * layers * 2 * n * feats * width,
        30 * 2**20,
        {3: 0},
    )


def pre_grad_kernel(where, pre_ref, own_ref, other_ref, out_ref, sum_ref):
    back = jax.vjp(smooth, pre_ref[...])[1]
    grad = back(own_ref[...] + other_ref[...])[0].astype(BF16)
    out_ref[...] = grad
    sum_ref[...] = jnp.sum(grad.astype(F32), axis=0, keepdims=True)


def enc_kernel(where, in_ref, grad_ref, *refs):
    *last, out_ref = refs
    out = lax.dot_general(
        in_ref[...], grad_ref[...], (((0,), (0,)), ((), ())), preferred_element_type=F32
    )
    out_ref[...] = last[0][...] + out if last else out


def enc_add(where, inputs, grad, last=None, steps=3):
    rows, width = inputs.shape
    feats = grad.shape[1]
    tile = pl.BlockSpec((width // steps, feats), lambda k, w: (k, 0))
    more = [] if last is None else [last]
    return call(
        enc_kernel,
        where,
        (inputs, grad, *more),
        [pl.BlockSpec((rows, width // steps), lambda k, w: (0, k)), fixed(rows, feats)] + [tile] * len(more),
        [((width, feats), F32)],
        [tile],
        steps,
        [],
        2 * rows * width * feats,
        4 * 2**20,
        {3: 0} if more else None,
    )[0]


def on_device(resid_in, resid_out, enc_weight, enc_bias, dec_weight, dec_bias):
    s, x, z, c = (lax.axis_index(a) for a in (LAYER, LX, LZ, TOK))
    ring = lax.axis_size(LX)
    layers, feats, model = dec_weight.shape[1:]
    tok = resid_in.shape[1]
    width = model // 2
    piece = tok // (ring * ring)
    scale = 1.0 / math.sqrt(tok * lax.axis_size(TOK))
    where = jnp.stack([s, c, x, z]).astype(jnp.int32)
    inputs, weights = resid_in[0], dec_weight[0]

    def mine_first(rows):
        blocks = rows.reshape(ring, ring, piece, rows.shape[1])
        return turned(turned(blocks, 0, x), 1, z).reshape(rows.shape)

    def crossed(rows):
        blocks = rows.reshape(ring, ring, -1, rows.shape[1])
        return blocks.transpose(1, 0, 2, 3).reshape(rows.shape)

    pre, own_lat = encode(where, inputs, enc_weight[0], enc_bias, ring)
    other_lat = crossed(swap(own_lat))

    part_a = rebuild(where, own_lat, weights, width)
    part_b = rebuild(where, other_lat, weights, width)
    a, b = ring_spread(*part_a, LX), ring_spread(*part_b, LZ)

    out_in, _ = lax.optimization_barrier((resid_out[0], part_b[3]))
    own_base = out_in.reshape(ring * ring, piece, -1)
    base = jnp.stack([own_base, swap(own_base)]).astype(F32)
    base = lax.all_to_all(dec_bias[0] - base, (LX, LZ), 1, 1, tiled=True)
    base = lax.dynamic_slice_in_dim(base, c * (ring * ring // 2), ring * ring // 2, 1)
    base = base.transpose(0, 2, 1, 3).reshape(2, piece, width)

    a, b = (v.reshape(layers, ring, piece, width) for v in (a, b))
    a = total(spread([a[:, 0]] + [a[:, i].astype(BF16) for i in range(1, ring)], LZ))
    b = total(spread([b[:, 0]] + [b[:, i].astype(BF16) for i in range(1, ring)], LX))
    pieces = jnp.stack([a, b], 1)
    rebuilt = pieces[0] + base
    for k in range(1, layers):
        rebuilt = rebuilt + send_up(pieces[k].astype(BF16), k).astype(F32)
    errors = (rebuilt * scale).astype(BF16)

    errors = jnp.stack([errors] + [send_up(errors, -k) for k in range(1, layers)], 1)
    near_a, far_a = ring_gather(jnp.concatenate(gathered(errors[0], LZ), 1), LX)
    near_b, far_b = ring_gather(jnp.concatenate(gathered(errors[1], LX), 1), LZ)

    ordered = mine_first(inputs)
    own_in = lax.dynamic_slice_in_dim(ordered, c * width, width, 1)
    other_in = swap(lax.dynamic_slice_in_dim(ordered, (1 - c) * width, width, 1))
    lat = jnp.concatenate([own_lat, other_lat], 0)
    own_in, other_in, *near = lax.optimization_barrier((own_in, other_in, *near_a, *near_b))

    dec_grad, own_act, other_act, sums = grads(
        where, lat, weights, near, far_a + far_b, width, ring
    )
    pre_grad, own_sum = call(
        pre_grad_kernel,
        where,
        (pre, own_act, swap(other_act)),
        [fixed(tok, feats)] * 3,
        [((tok, feats), BF16), ((1, feats), F32)],
        [fixed(tok, feats), fixed(1, feats)],
        1,
        [],
        20 * tok * feats,
        4 * 2**20,
    )
    enc_grad = enc_add(where, own_in, pre_grad)
    enc_grad = enc_add(where, other_in, swap(pre_grad), enc_grad)
    enc_bias_grad = own_sum + swap(own_sum)
    both = turned(jnp.concatenate([sums, swap(sums)], 0), 0, c).reshape(1, model)
    size = dec_bias.shape[1]
    dec_bias_grad = lax.dynamic_slice_in_dim(both, (x * ring + z) * size, size, 1)
    return dec_grad[None], dec_bias_grad, enc_grad[None], enc_bias_grad


def solution(mesh):
    ring = math.isqrt(mesh.shape["latent"])
    shape = (mesh.shape["layer"], ring, ring, mesh.shape["tok"])
    fine = jax.sharding.Mesh(mesh.devices.reshape(shape), (LAYER, LX, LZ, TOK))
    latent = (LX, LZ)
    in_specs = (
        P(LAYER, TOK, None),
        P(LAYER, TOK, latent),
        P(LAYER, None, latent),
        P(LAYER, latent),
        P(LAYER, None, latent, None),
        P(LAYER, latent),
    )
    out_specs = (
        P(LAYER, None, latent, TOK),
        P(LAYER, latent),
        P(LAYER, TOK, latent),
        P(LAYER, latent),
    )
    return jax.shard_map(
        on_device, mesh=fine, in_specs=in_specs, out_specs=out_specs, check_vma=False
    )
```

```python
import functools
import math

import jax
import jax.numpy as jnp
from jax import lax
from jax.experimental import pallas as pl
from jax.experimental.pallas import tpu as pltpu
from jax.sharding import PartitionSpec as P

LAYER, LX, LZ, TOK = "layer", "lx", "lz", "tok"
BF16, F32 = jnp.bfloat16, jnp.float32
VMEM_MIB = 28


def smooth(values):
    return jax.nn.gelu(values, approximate=True)


def shift(value, axis, step):
    n = lax.axis_size(axis)
    return lax.ppermute(value, axis, [(i, (i + step) % n) for i in range(n)])


def send_up(value, step):
    n = lax.axis_size(LAYER)
    pairs = [(i, i + step) for i in range(n) if 0 <= i + step < n]
    return lax.ppermute(value, LAYER, pairs)


def swap(value):
    return lax.ppermute(value, TOK, [(0, 1), (1, 0)])


def turned(value, axis, by):
    n = value.shape[axis]
    return lax.dynamic_slice_in_dim(jnp.concatenate([value, value], axis), by, n, axis)


def total(values):
    return functools.reduce(jnp.add, [v.astype(F32) for v in values])


def spread(value, axis):
    return [value[0]] + [shift(value[k], axis, k) for k in range(1, len(value))]


def gathered(value, axis):
    n = lax.axis_size(axis)
    return [value] + [shift(value, axis, -k) for k in range(1, n)]


def call(kernel, where, inputs, in_specs, outs, out_specs, grid, scratch, flops, moved, aliases=None):
    return pl.pallas_call(
        kernel,
        out_shape=[jax.ShapeDtypeStruct(shape, dtype) for shape, dtype in outs],
        grid_spec=pltpu.PrefetchScalarGridSpec(
            num_scalar_prefetch=1,
            grid=(grid,),
            in_specs=in_specs,
            out_specs=out_specs,
            scratch_shapes=scratch,
        ),
        input_output_aliases=aliases or {},
        compiler_params=pltpu.CompilerParams(vmem_limit_bytes=VMEM_MIB * 2**20),
        cost_estimate=pl.CostEstimate(flops=flops, bytes_accessed=moved, transcendentals=0),
    )(where, *inputs)


def fixed(*shape):
    return pl.BlockSpec(shape, lambda k, w: (0,) * len(shape))


def each(*shape):
    return pl.BlockSpec(shape, lambda k, w: (k,) + (0,) * (len(shape) - 1))


def encode_kernel(where, in_ref, w_ref, bias_ref, pre_ref, lat_ref, turned_ref, acc_ref, *, ring):
    k = pl.program_id(0)

    @pl.when(k == 0)
    def _():
        acc_ref[...] = jnp.broadcast_to(bias_ref[...], acc_ref.shape)

    acc_ref[...] += jnp.dot(in_ref[...], w_ref[...], preferred_element_type=F32)

    @pl.when(k == pl.num_programs(0) - 1)
    def _():
        piece = acc_ref.shape[0] // (ring * ring)
        for i in range(ring):
            for j in range(ring):
                row, col = lax.rem(i + ring - where[2], ring), lax.rem(j + ring - where[3], ring)
                pre = acc_ref[(i * ring + j) * piece : (i * ring + j + 1) * piece, :]
                latent = smooth(pre).astype(BF16)
                to = pl.ds(pl.multiple_of((row * ring + col) * piece, piece), piece)
                pre_ref[to, :] = pre
                lat_ref[to, :] = latent
                turned_ref[pl.ds(pl.multiple_of((col * ring + row) * piece, piece), piece), :] = latent


def encode(where, inputs, weight, bias, ring, steps=3):
    rows, model = inputs.shape
    feats = weight.shape[1]
    return call(
        functools.partial(encode_kernel, ring=ring),
        where,
        (inputs, weight, bias),
        [
            pl.BlockSpec((rows, model // steps), lambda k, w: (0, k)),
            pl.BlockSpec((model // steps, feats), lambda k, w: (k, 0)),
            fixed(1, feats),
        ],
        [((rows, feats), F32), ((rows, feats), BF16), ((rows, feats), BF16)],
        [fixed(rows, feats)] * 3,
        steps,
        [pltpu.VMEM((rows, feats), F32)],
        2 * rows * model * feats,
        8 * 2**20,
    )


def far_kernel(where, own_ref, other_ref, w_ref, *out_refs):
    for lat_ref, refs in ((own_ref, out_refs[:2]), (other_ref, out_refs[2:])):
        n = lat_ref.shape[0] // 4
        out = jnp.dot(lat_ref[2 * n : 3 * n, :], w_ref[0], preferred_element_type=F32).astype(BF16)
        refs[0][0] = out[: n // 2]
        refs[1][0] = out[n // 2 :]


def near_kernel(where, own_ref, other_ref, w_ref, *out_refs):
    for lat_ref, refs in ((own_ref, out_refs[:3]), (other_ref, out_refs[3:])):
        n = lat_ref.shape[0] // 4
        out = jnp.dot(lat_ref[: 2 * n, :], w_ref[0], preferred_element_type=F32)
        refs[0][0] = out[:n]
        refs[1][0] = out[n:].astype(BF16)
        out = jnp.dot(lat_ref[3 * n :, :], w_ref[0], preferred_element_type=F32)
        refs[2][0] = out.astype(BF16)


def rebuild(kernel, where, own_lat, other_lat, weights, width):
    layers, feats, _ = weights.shape
    rows = own_lat.shape[0]
    n = rows // 4
    half = ((layers, n // 2, width), BF16)
    if kernel is far_kernel:
        outs, used = [half] * 4, 2 * n
    else:
        outs, used = [((layers, n, width), d) for d in (F32, BF16, BF16)] * 2, 6 * n
    return call(
        kernel,
        where,
        (own_lat, other_lat, weights),
        [
            fixed(rows, feats),
            fixed(rows, feats),
            pl.BlockSpec((1, feats, width), lambda k, w: (lax.rem(w[0] + k, layers), 0, 0)),
        ],
        outs,
        [each(1, *shape[1:]) for shape, _ in outs],
        layers,
        [],
        2 * layers * used * feats * width,
        8 * 2**20,
    )


def fold_kernel(where, *refs):
    for i in range(4):
        value, rows, out = refs[i], refs[4 + i], refs[8 + i]
        out[...] = (value[...].astype(F32) + rows[...].astype(F32)).astype(BF16)


def fold(where, values, rows, steps=2):
    layers, n, width = values[0].shape
    half = (layers // steps, n // 2, width)
    low, high = pl.BlockSpec(half, lambda k, w: (k, 0, 0)), pl.BlockSpec(half, lambda k, w: (k, 1, 0))
    return call(
        fold_kernel,
        where,
        (*values, *rows),
        [low, high, low, high] + [each(*half)] * 4,
        [(v.shape, BF16) for v in values],
        [low, high, low, high],
        steps,
        [],
        4 * values[0].size,
        12 * values[0].size,
        {1 + i: i for i in range(4)},
    )


def near_act_kernel(where, w_ref, *refs):
    *x_refs, act_ref, err_ref = refs
    k = pl.program_id(0)
    step = x_refs[0].shape[1]

    @pl.when(k == 0)
    def _():
        act_ref[...] = jnp.zeros_like(act_ref)

    @pl.when(where[0] + k < pl.num_programs(0))
    def _():
        for i, x_ref in enumerate(x_refs):
            err_ref[i * step : (i + 1) * step, :] = x_ref[0]
        for i in range(0, err_ref.shape[0], 256):
            act_ref[i : i + 256, :] += lax.dot_general(
                err_ref[i : i + 256, :], w_ref[0], (((1,), (1,)), ((), ())), preferred_element_type=F32
            )


def far_act_kernel(where, w_ref, near_ref, *refs, ring):
    *x_refs, own_ref, other_ref, err_ref, act_ref = refs
    k = pl.program_id(0)
    step = x_refs[0].shape[1]

    @pl.when(k == 0)
    def _():
        act_ref[...] = jnp.zeros_like(act_ref)

    @pl.when(where[0] + k < pl.num_programs(0))
    def _():
        for i, x_ref in enumerate(x_refs):
            err_ref[i * step : (i + 1) * step, :] = x_ref[0]
        act_ref[...] += lax.dot_general(
            err_ref[...], w_ref[0], (((1,), (1,)), ((), ())), preferred_element_type=F32
        )

    @pl.when(k == pl.num_programs(0) - 1)
    def _():
        n = act_ref.shape[0] // 2
        piece = n // ring
        for side in range(2):
            for i in range(ring):
                ref, at = {
                    0: (near_ref, 3 * n * side),
                    1: (near_ref, 3 * n * side + n),
                    2: (act_ref, n * side),
                    3: (near_ref, 3 * n * side + 2 * n),
                }[i]
                if side == 0:
                    own_ref[i * n : (i + 1) * n, :] = ref[at : at + n, :]
                else:
                    for j in range(ring):
                        to = (j * ring + i) * piece
                        other_ref[to : to + piece, :] = ref[at + j * piece : at + (j + 1) * piece, :]


def act_grads(where, weights, near, far, width, ring):
    layers, feats, _ = weights.shape
    n = near[0].shape[1]
    target = pl.BlockSpec((1, feats, width), lambda k, w: (lax.rem(w[0] + k, layers), 0, 0))
    [act] = call(
        near_act_kernel,
        where,
        (weights, *near),
        [target] + [each(1, n, width)] * 6,
        [((6 * n, feats), F32)],
        [fixed(6 * n, feats)],
        layers,
        [pltpu.VMEM((6 * n, width), BF16)],
        2 * layers * 6 * n * feats * width,
        14 * 2**20,
    )
    return call(
        functools.partial(far_act_kernel, ring=ring),
        where,
        (weights, act, *far),
        [target, fixed(6 * n, feats)] + [each(1, n // 2, width)] * 4,
        [((4 * n, feats), F32)] * 2,
        [fixed(4 * n, feats)] * 2,
        layers,
        [pltpu.VMEM((2 * n, width), BF16), pltpu.VMEM((2 * n, feats), F32)],
        2 * layers * 2 * n * feats * width,
        10 * 2**20,
    )


def dec_kernel(where, own_ref, other_ref, *refs):
    *x_refs, dec_ref, sum_ref, err_ref = refs
    live = where[0] + pl.program_id(0) < pl.num_programs(0)
    rows = own_ref.shape[0]

    @pl.when(live)
    def _():
        half = x_refs[-1].shape[1]
        starts = [0, 2, 6, 8, 10, 14, 4, 5, 12, 13]
        for x_ref, start in zip(x_refs, starts, strict=True):
            err_ref[start * half : start * half + x_ref.shape[1], :] = x_ref[0]
        dims = (((0,), (0,)), ((), ()))
        dec_ref[0] = lax.dot_general(
            own_ref[...], err_ref[:rows, :], dims, preferred_element_type=F32
        ) + lax.dot_general(other_ref[...], err_ref[rows:, :], dims, preferred_element_type=F32)

    @pl.when(jnp.logical_not(live))
    def _():
        dec_ref[0] = jnp.zeros_like(dec_ref[0])

    @pl.when(pl.program_id(0) == 0)
    def _():
        sum_ref[...] = jnp.sum(err_ref[...].astype(F32), axis=0, keepdims=True)


def dec_gradient(where, own_lat, other_lat, errs):
    rows, feats = own_lat.shape
    layers, _, width = errs[0].shape
    return call(
        dec_kernel,
        where,
        (own_lat, other_lat, *errs),
        [fixed(rows, feats)] * 2 + [each(1, e.shape[1], width) for e in errs],
        [((layers, feats, width), F32), ((1, width), F32)],
        [
            pl.BlockSpec((1, feats, width), lambda k, w: (lax.rem(w[0] + k, layers), 0, 0)),
            fixed(1, width),
        ],
        layers,
        [pltpu.VMEM((2 * rows, width), BF16)],
        4 * layers * rows * feats * width,
        20 * 2**20,
    )


def enc_kernel(where, in_ref, other_ref, grad_ref, other_grad_ref, out_ref):
    out_ref[...] = jnp.dot(in_ref[...], grad_ref[...], preferred_element_type=F32) + jnp.dot(
        other_ref[...], other_grad_ref[...], preferred_element_type=F32
    )


def enc_gradient(where, own_t, other_t, grad, other_grad, steps=6):
    width, rows = own_t.shape
    feats = grad.shape[1]
    tile = pl.BlockSpec((width // steps, rows), lambda k, w: (k, 0))
    return call(
        enc_kernel,
        where,
        (own_t, other_t, grad, other_grad),
        [tile, tile, fixed(rows, feats), fixed(rows, feats)],
        [((width, feats), F32)],
        [pl.BlockSpec((width // steps, feats), lambda k, w: (k, 0))],
        steps,
        [],
        4 * rows * width * feats,
        6 * 2**20,
    )[0]


def on_device(resid_in, resid_out, enc_weight, enc_bias, dec_weight, dec_bias):
    s, x, z, c = (lax.axis_index(a) for a in (LAYER, LX, LZ, TOK))
    ring = lax.axis_size(LX)
    layers, feats, model = dec_weight.shape[1:]
    tok = resid_in.shape[1]
    width = model // 2
    piece = tok // (ring * ring)
    scale = 1.0 / math.sqrt(tok * lax.axis_size(TOK))
    where = jnp.stack([s, c, x, z]).astype(jnp.int32)
    inputs = resid_in[0]
    weights = lax.dynamic_slice_in_dim(dec_weight[0], c * width, width, 2)

    def mine_first(rows):
        blocks = rows.reshape(ring, ring, piece, rows.shape[1])
        return turned(turned(blocks, 0, x), 1, z).reshape(rows.shape)

    pre, own_lat, crossed = encode(where, inputs, enc_weight[0], enc_bias, ring)
    own_out = resid_out[0].reshape(ring * ring, piece, -1)
    other_lat, other_out = lax.optimization_barrier((swap(crossed), swap(own_out)))

    far_a0, far_a1, far_b0, far_b1 = rebuild(far_kernel, where, own_lat, other_lat, weights, width)
    parts = [(far_a0, LX, 1), (far_a1, LX, -1), (far_b0, LZ, 1), (far_b1, LZ, -1)]
    got = [shift(*part) for part in parts]
    own_a, up_a, down_a, own_b, up_b, down_b = rebuild(
        near_kernel, where, own_lat, other_lat, weights, width
    )
    folded = fold(where, (up_a, down_a, up_b, down_b), got)
    got = [shift(value, *part[1:]) for value, part in zip(folded, parts, strict=True)]

    later, *_ = lax.optimization_barrier((inputs, *folded))
    ordered = mine_first(later)
    own_in = lax.dynamic_slice_in_dim(ordered, c * width, width, 1)
    to_other = lax.dynamic_slice_in_dim(ordered, (1 - c) * width, width, 1)
    own_in = own_in.T

    own_out, other_out, own_in, to_other = lax.optimization_barrier(
        (own_out, other_out, own_in, to_other)
    )
    base = dec_bias[0] - jnp.stack([own_out, other_out], 1).astype(F32)
    base = lax.all_to_all(base, (LX, LZ), 0, 0, tiled=True)
    base = lax.dynamic_slice_in_dim(base, c * (ring * ring // 2), ring * ring // 2, 0)
    base = base.transpose(1, 2, 0, 3).reshape(2, piece, width)

    a = total([own_a, *got[:2]]).reshape(layers, ring, piece, width)
    b = total([own_b, *got[2:]]).reshape(layers, ring, piece, width)
    a = spread([a[:, 0]] + [a[:, i].astype(BF16) for i in range(1, ring)], LZ)
    b = spread([b[:, 0]] + [b[:, i].astype(BF16) for i in range(1, ring)], LX)
    base, b[3] = lax.optimization_barrier((base, b[3]))
    a, b = total(a), total(b)
    pieces = jnp.stack([a, b], 1)
    rebuilt = pieces[0] + base
    for k in range(1, layers):
        rebuilt = rebuilt + send_up(pieces[k].astype(BF16), k).astype(F32)
    errors = (rebuilt * scale).astype(BF16)

    errors, to_other = lax.optimization_barrier((errors, to_other))
    other_in = swap(to_other).T
    errors = jnp.stack([errors] + [send_up(errors, -k) for k in range(1, layers)], 1)
    paths = [(LX, -1), (LX, 1), (LZ, -1), (LZ, 1)]
    own_a = jnp.concatenate(gathered(errors[0], LZ), 1)
    own_b = jnp.concatenate(gathered(errors[1], LX), 1)
    got = [shift(v, *path) for v, path in zip((own_a, own_a, own_b, own_b), paths, strict=True)]
    half = got[0].shape[1] // 2
    far = [
        shift(v[:, i % 2 * half : (i % 2 + 1) * half], *path)
        for i, (v, path) in enumerate(zip(got, paths, strict=True))
    ]
    own_in, other_in, *got = lax.optimization_barrier((own_in, other_in, *got))
    near = [own_a, *got[:2], own_b, *got[2:]]

    own_act, other_act = act_grads(where, weights, near, far, width, ring)
    dec_grad, sums = dec_gradient(where, own_lat, other_lat, [*near, *far])
    pre, sums = lax.optimization_barrier((pre, sums))
    act = own_act + swap(other_act)
    pre_grad = jax.vjp(smooth, pre)[1](act)[0].astype(BF16)
    own_sum = jnp.sum(pre_grad.astype(F32), axis=0, keepdims=True)
    enc_grad = enc_gradient(where, own_in, other_in, pre_grad, swap(pre_grad))
    enc_bias_grad = own_sum + swap(own_sum)
    both = turned(jnp.concatenate([sums, swap(sums)], 0), 0, c).reshape(1, model)
    size = dec_bias.shape[1]
    dec_bias_grad = lax.dynamic_slice_in_dim(both, (x * ring + z) * size, size, 1)
    return dec_grad[None], dec_bias_grad, enc_grad[None], enc_bias_grad


def solution(mesh):
    ring = math.isqrt(mesh.shape["latent"])
    shape = (mesh.shape["layer"], ring, ring, mesh.shape["tok"])
    fine = jax.sharding.Mesh(mesh.devices.reshape(shape), (LAYER, LX, LZ, TOK))
    latent = (LX, LZ)
    in_specs = (
        P(LAYER, TOK, None),
        P(LAYER, TOK, latent),
        P(LAYER, None, latent),
        P(LAYER, latent),
        P(LAYER, None, latent, None),
        P(LAYER, latent),
    )
    out_specs = (
        P(LAYER, None, latent, TOK),
        P(LAYER, latent),
        P(LAYER, TOK, latent),
        P(LAYER, latent),
    )
    return jax.shard_map(
        on_device, mesh=fine, in_specs=in_specs, out_specs=out_specs, check_vma=False
    )
```

```python
import functools
import math

import jax
import jax.numpy as jnp
from jax import lax
from jax.experimental import pallas as pl
from jax.experimental.pallas import tpu as pltpu
from jax.sharding import PartitionSpec as P

LAYER, LX, LZ, TOK = "layer", "lx", "lz", "tok"
BF16, F32 = jnp.bfloat16, jnp.float32
VMEM_MIB, LARGE_MIB = 28, 56


def smooth(values):
    return jax.nn.gelu(values, approximate=True)


def shift(value, axis, step):
    n = lax.axis_size(axis)
    return lax.ppermute(value, axis, [(i, (i + step) % n) for i in range(n)])


def send_up(value, step):
    n = lax.axis_size(LAYER)
    pairs = [(i, i + step) for i in range(n) if 0 <= i + step < n]
    return lax.ppermute(value, LAYER, pairs)


def swap(value):
    return lax.ppermute(value, TOK, [(0, 1), (1, 0)])


def turned(value, axis, by):
    n = value.shape[axis]
    return lax.dynamic_slice_in_dim(jnp.concatenate([value, value], axis), by, n, axis)


def total(values):
    return functools.reduce(jnp.add, [v.astype(F32) for v in values])


def spread(value, axis):
    return [value[0]] + [shift(value[k], axis, k) for k in range(1, len(value))]


def gathered(value, axis):
    n = lax.axis_size(axis)
    return [value] + [shift(value, axis, -k) for k in range(1, n)]


def call(kernel, where, inputs, in_specs, outs, out_specs, grid, scratch, flops, moved, aliases=None, mib=VMEM_MIB):
    return pl.pallas_call(
        kernel,
        out_shape=[jax.ShapeDtypeStruct(shape, dtype) for shape, dtype in outs],
        grid_spec=pltpu.PrefetchScalarGridSpec(
            num_scalar_prefetch=1,
            grid=(grid,),
            in_specs=in_specs,
            out_specs=out_specs,
            scratch_shapes=scratch,
        ),
        input_output_aliases=aliases or {},
        compiler_params=pltpu.CompilerParams(vmem_limit_bytes=mib * 2**20),
        cost_estimate=pl.CostEstimate(flops=flops, bytes_accessed=moved, transcendentals=0),
    )(where, *inputs)


def fixed(*shape):
    return pl.BlockSpec(shape, lambda k, w: (0,) * len(shape))


def each(*shape):
    return pl.BlockSpec(shape, lambda k, w: (k,) + (0,) * (len(shape) - 1))


def encode_kernel(where, in_ref, w_ref, bias_ref, pre_ref, lat_ref, turned_ref, acc_ref, *, ring):
    k = pl.program_id(0)

    @pl.when(k == 0)
    def _():
        acc_ref[...] = jnp.broadcast_to(bias_ref[...], acc_ref.shape)

    acc_ref[...] += jnp.dot(in_ref[...], w_ref[...], preferred_element_type=F32)

    @pl.when(k == pl.num_programs(0) - 1)
    def _():
        piece = acc_ref.shape[0] // (ring * ring)
        for i in range(ring):
            for j in range(ring):
                row, col = lax.rem(i + ring - where[2], ring), lax.rem(j + ring - where[3], ring)
                pre = acc_ref[(i * ring + j) * piece : (i * ring + j + 1) * piece, :]
                latent = smooth(pre).astype(BF16)
                to = pl.ds(pl.multiple_of((row * ring + col) * piece, piece), piece)
                pre_ref[to, :] = pre
                lat_ref[to, :] = latent
                turned_ref[pl.ds(pl.multiple_of((col * ring + row) * piece, piece), piece), :] = latent


def encode(where, inputs, weight, bias, ring, steps=3):
    rows, model = inputs.shape
    feats = weight.shape[1]
    return call(
        functools.partial(encode_kernel, ring=ring),
        where,
        (inputs, weight, bias),
        [
            pl.BlockSpec((rows, model // steps), lambda k, w: (0, k)),
            pl.BlockSpec((model // steps, feats), lambda k, w: (k, 0)),
            fixed(1, feats),
        ],
        [((rows, feats), F32), ((rows, feats), BF16), ((rows, feats), BF16)],
        [fixed(rows, feats)] * 3,
        steps,
        [pltpu.VMEM((rows, feats), F32)],
        2 * rows * model * feats,
        8 * 2**20,
    )


def far_kernel(where, own_ref, other_ref, w_ref, *out_refs):
    for lat_ref, refs in ((own_ref, out_refs[:2]), (other_ref, out_refs[2:])):
        n = lat_ref.shape[0] // 4
        out = jnp.dot(lat_ref[2 * n : 3 * n, :], w_ref[0], preferred_element_type=F32).astype(BF16)
        refs[0][0] = out[: n // 2]
        refs[1][0] = out[n // 2 :]


def near_kernel(where, own_ref, other_ref, w_ref, *out_refs):
    for lat_ref, refs in ((own_ref, out_refs[:3]), (other_ref, out_refs[3:])):
        n = lat_ref.shape[0] // 4
        out = jnp.dot(lat_ref[: 2 * n, :], w_ref[0], preferred_element_type=F32)
        refs[0][0] = out[:n]
        refs[1][0] = out[n:].astype(BF16)
        out = jnp.dot(lat_ref[3 * n :, :], w_ref[0], preferred_element_type=F32)
        refs[2][0] = out.astype(BF16)


def rebuild(kernel, where, own_lat, other_lat, weights, width):
    layers, feats, _ = weights.shape
    rows = own_lat.shape[0]
    n = rows // 4
    half = ((layers, n // 2, width), BF16)
    if kernel is far_kernel:
        outs, used = [half] * 4, 2 * n
    else:
        outs, used = [((layers, n, width), d) for d in (F32, BF16, BF16)] * 2, 6 * n
    return call(
        kernel,
        where,
        (own_lat, other_lat, weights),
        [
            fixed(rows, feats),
            fixed(rows, feats),
            pl.BlockSpec((1, feats, width), lambda k, w: (lax.rem(w[0] + k, layers), 0, 0)),
        ],
        outs,
        [each(1, *shape[1:]) for shape, _ in outs],
        layers,
        [],
        2 * layers * used * feats * width,
        8 * 2**20,
        mib=VMEM_MIB if kernel is far_kernel else LARGE_MIB,
    )


def fold_kernel(where, *refs):
    for i in range(4):
        value, rows, out = refs[i], refs[4 + i], refs[8 + i]
        out[...] = (value[...].astype(F32) + rows[...].astype(F32)).astype(BF16)


def fold(where, values, rows, steps=2):
    layers, n, width = values[0].shape
    half = (layers // steps, n // 2, width)
    low, high = pl.BlockSpec(half, lambda k, w: (k, 0, 0)), pl.BlockSpec(half, lambda k, w: (k, 1, 0))
    return call(
        fold_kernel,
        where,
        (*values, *rows),
        [low, high, low, high] + [each(*half)] * 4,
        [(v.shape, BF16) for v in values],
        [low, high, low, high],
        steps,
        [],
        4 * values[0].size,
        12 * values[0].size,
        {1 + i: i for i in range(4)},
    )


def near_act_kernel(where, w_ref, *refs):
    *x_refs, act_ref, err_ref = refs
    k = pl.program_id(0)
    step = x_refs[0].shape[1]

    @pl.when(k == 0)
    def _():
        act_ref[...] = jnp.zeros_like(act_ref)

    @pl.when(where[0] + k < pl.num_programs(0))
    def _():
        for i, x_ref in enumerate(x_refs):
            err_ref[i * step : (i + 1) * step, :] = x_ref[0]
        for i in range(0, err_ref.shape[0], 256):
            act_ref[i : i + 256, :] += lax.dot_general(
                err_ref[i : i + 256, :], w_ref[0], (((1,), (1,)), ((), ())), preferred_element_type=F32
            )


def far_act_kernel(where, w_ref, near_ref, *refs, ring):
    *x_refs, own_ref, other_ref, err_ref, act_ref = refs
    k = pl.program_id(0)
    step = x_refs[0].shape[1]

    @pl.when(k == 0)
    def _():
        act_ref[...] = jnp.zeros_like(act_ref)

    @pl.when(where[0] + k < pl.num_programs(0))
    def _():
        for i, x_ref in enumerate(x_refs):
            err_ref[i * step : (i + 1) * step, :] = x_ref[0]
        act_ref[...] += lax.dot_general(
            err_ref[...], w_ref[0], (((1,), (1,)), ((), ())), preferred_element_type=F32
        )

    @pl.when(k == pl.num_programs(0) - 1)
    def _():
        n = act_ref.shape[0] // 2
        piece = n // ring
        for side in range(2):
            for i in range(ring):
                ref, at = {
                    0: (near_ref, 3 * n * side),
                    1: (near_ref, 3 * n * side + n),
                    2: (act_ref, n * side),
                    3: (near_ref, 3 * n * side + 2 * n),
                }[i]
                if side == 0:
                    own_ref[i * n : (i + 1) * n, :] = ref[at : at + n, :]
                else:
                    for j in range(ring):
                        to = (j * ring + i) * piece
                        other_ref[to : to + piece, :] = ref[at + j * piece : at + (j + 1) * piece, :]


def act_grads(where, weights, near, far, width, ring):
    layers, feats, _ = weights.shape
    n = near[0].shape[1]
    target = pl.BlockSpec((1, feats, width), lambda k, w: (lax.rem(w[0] + k, layers), 0, 0))
    [act] = call(
        near_act_kernel,
        where,
        (weights, *near),
        [target] + [each(1, n, width)] * 6,
        [((6 * n, feats), F32)],
        [fixed(6 * n, feats)],
        layers,
        [pltpu.VMEM((6 * n, width), BF16)],
        2 * layers * 6 * n * feats * width,
        14 * 2**20,
    )
    return call(
        functools.partial(far_act_kernel, ring=ring),
        where,
        (weights, act, *far),
        [target, fixed(6 * n, feats)] + [each(1, n // 2, width)] * 4,
        [((4 * n, feats), F32)] * 2,
        [fixed(4 * n, feats)] * 2,
        layers,
        [pltpu.VMEM((2 * n, width), BF16), pltpu.VMEM((2 * n, feats), F32)],
        2 * layers * 2 * n * feats * width,
        10 * 2**20,
    )


def dec_kernel(where, own_ref, other_ref, *refs):
    *x_refs, dec_ref, sum_ref, err_ref = refs
    live = where[0] + pl.program_id(0) < pl.num_programs(0)
    rows = own_ref.shape[0]

    @pl.when(live)
    def _():
        half = x_refs[-1].shape[1]
        starts = [0, 2, 6, 8, 10, 14, 4, 5, 12, 13]
        for x_ref, start in zip(x_refs, starts, strict=True):
            err_ref[start * half : start * half + x_ref.shape[1], :] = x_ref[0]
        dims = (((0,), (0,)), ((), ()))
        dec_ref[0] = lax.dot_general(
            own_ref[...], err_ref[:rows, :], dims, preferred_element_type=F32
        ) + lax.dot_general(other_ref[...], err_ref[rows:, :], dims, preferred_element_type=F32)

    @pl.when(jnp.logical_not(live))
    def _():
        dec_ref[0] = jnp.zeros_like(dec_ref[0])

    @pl.when(pl.program_id(0) == 0)
    def _():
        sum_ref[...] = jnp.sum(err_ref[...].astype(F32), axis=0, keepdims=True)


def dec_gradient(where, own_lat, other_lat, errs):
    rows, feats = own_lat.shape
    layers, _, width = errs[0].shape
    return call(
        dec_kernel,
        where,
        (own_lat, other_lat, *errs),
        [fixed(rows, feats)] * 2 + [each(1, e.shape[1], width) for e in errs],
        [((layers, feats, width), F32), ((1, width), F32)],
        [
            pl.BlockSpec((1, feats, width), lambda k, w: (lax.rem(w[0] + k, layers), 0, 0)),
            fixed(1, width),
        ],
        layers,
        [pltpu.VMEM((2 * rows, width), BF16)],
        4 * layers * rows * feats * width,
        20 * 2**20,
    )


def enc_kernel(where, in_ref, other_ref, grad_ref, other_grad_ref, out_ref):
    out_ref[...] = jnp.dot(in_ref[...], grad_ref[...], preferred_element_type=F32) + jnp.dot(
        other_ref[...], other_grad_ref[...], preferred_element_type=F32
    )


def enc_gradient(where, own_t, other_t, grad, other_grad, steps=6):
    width, rows = own_t.shape
    feats = grad.shape[1]
    tile = pl.BlockSpec((width // steps, rows), lambda k, w: (k, 0))
    return call(
        enc_kernel,
        where,
        (own_t, other_t, grad, other_grad),
        [tile, tile, fixed(rows, feats), fixed(rows, feats)],
        [((width, feats), F32)],
        [pl.BlockSpec((width // steps, feats), lambda k, w: (k, 0))],
        steps,
        [],
        4 * rows * width * feats,
        6 * 2**20,
    )[0]


def on_device(resid_in, resid_out, enc_weight, enc_bias, dec_weight, dec_bias):
    s, x, z, c = (lax.axis_index(a) for a in (LAYER, LX, LZ, TOK))
    ring = lax.axis_size(LX)
    layers, feats, model = dec_weight.shape[1:]
    tok = resid_in.shape[1]
    width = model // 2
    piece = tok // (ring * ring)
    scale = 1.0 / math.sqrt(tok * lax.axis_size(TOK))
    where = jnp.stack([s, c, x, z]).astype(jnp.int32)
    inputs = resid_in[0]
    weights = lax.dynamic_slice_in_dim(dec_weight[0], c * width, width, 2)

    def mine_first(rows):
        blocks = rows.reshape(ring, ring, piece, rows.shape[1])
        return turned(turned(blocks, 0, x), 1, z).reshape(rows.shape)

    pre, own_lat, crossed = encode(where, inputs, enc_weight[0], enc_bias, ring)
    other_lat = swap(crossed)

    far_a0, far_a1, far_b0, far_b1 = rebuild(far_kernel, where, own_lat, other_lat, weights, width)
    parts = [(far_a0, LX, 1), (far_a1, LX, -1), (far_b0, LZ, 1), (far_b1, LZ, -1)]
    got = [shift(*part) for part in parts]
    own_a, up_a, down_a, own_b, up_b, down_b = rebuild(
        near_kernel, where, own_lat, other_lat, weights, width
    )
    out_in, own_a = lax.optimization_barrier((resid_out[0], own_a))
    base = dec_bias[0] - out_in.astype(F32).reshape(ring * ring, piece, -1)
    base = lax.all_to_all(base, (LX, LZ), 0, 0, tiled=True)
    folded = fold(where, (up_a, down_a, up_b, down_b), got)
    got = [shift(value, *part[1:]) for value, part in zip(folded, parts, strict=True)]

    later, *_ = lax.optimization_barrier((inputs, *folded))
    ordered = mine_first(later)
    own_in = lax.dynamic_slice_in_dim(ordered, c * width, width, 1)
    to_other = lax.dynamic_slice_in_dim(ordered, (1 - c) * width, width, 1)
    own_in = own_in.T

    base, own_in, to_other = lax.optimization_barrier((base, own_in, to_other))
    halves = base.reshape(2, ring * ring // 2, piece, -1)
    own_base, other_base = (
        lax.dynamic_index_in_dim(halves, core, 0, False).transpose(1, 0, 2).reshape(piece, width)
        for core in (c, 1 - c)
    )
    base = jnp.stack([own_base, swap(other_base)])

    def settled(own, below, above):
        cuts = [slice(i * piece, (i + 1) * piece) for i in range(ring)]
        sums = [total([v[:, cut] for v in (own, below, above)]) for cut in cuts]
        return [sums[0]] + [v.astype(BF16) for v in sums[1:]]

    a = spread(settled(own_a, *got[:2]), LZ)
    b = spread(settled(own_b, *got[2:]), LX)
    base, b[3] = lax.optimization_barrier((base, b[3]))
    a, b = total(a), total(b)
    pieces = jnp.stack([a, b], 1)
    rebuilt = pieces[0] + base
    for k in range(1, layers):
        rebuilt = rebuilt + send_up(pieces[k].astype(BF16), k).astype(F32)
    errors = (rebuilt * scale).astype(BF16)

    errors, to_other = lax.optimization_barrier((errors, to_other))
    other_in = swap(to_other).T
    errors = jnp.stack([errors] + [send_up(errors, -k) for k in range(1, layers)], 1)
    paths = [(LX, -1), (LX, 1), (LZ, -1), (LZ, 1)]
    own_a = jnp.concatenate(gathered(errors[0], LZ), 1)
    own_b = jnp.concatenate(gathered(errors[1], LX), 1)
    got = [shift(v, *path) for v, path in zip((own_a, own_a, own_b, own_b), paths, strict=True)]
    half = got[0].shape[1] // 2
    far = [
        shift(v[:, i % 2 * half : (i % 2 + 1) * half], *path)
        for i, (v, path) in enumerate(zip(got, paths, strict=True))
    ]
    own_in, other_in, *got = lax.optimization_barrier((own_in, other_in, *got))
    near = [own_a, *got[:2], own_b, *got[2:]]

    own_act, other_act = act_grads(where, weights, near, far, width, ring)
    dec_grad, sums = dec_gradient(where, own_lat, other_lat, [*near, *far])
    pre, sums = lax.optimization_barrier((pre, sums))
    act = own_act + swap(other_act)
    pre_grad = jax.vjp(smooth, pre)[1](act)[0].astype(BF16)
    own_sum = jnp.sum(pre_grad.astype(F32), axis=0, keepdims=True)
    enc_grad = enc_gradient(where, own_in, other_in, pre_grad, swap(pre_grad))
    enc_bias_grad = own_sum + swap(own_sum)
    both = turned(jnp.concatenate([sums, swap(sums)], 0), 0, c).reshape(1, model)
    size = dec_bias.shape[1]
    dec_bias_grad = lax.dynamic_slice_in_dim(both, (x * ring + z) * size, size, 1)
    return dec_grad[None], dec_bias_grad, enc_grad[None], enc_bias_grad


def solution(mesh):
    ring = math.isqrt(mesh.shape["latent"])
    shape = (mesh.shape["layer"], ring, ring, mesh.shape["tok"])
    fine = jax.sharding.Mesh(mesh.devices.reshape(shape), (LAYER, LX, LZ, TOK))
    latent = (LX, LZ)
    in_specs = (
        P(LAYER, TOK, None),
        P(LAYER, TOK, latent),
        P(LAYER, None, latent),
        P(LAYER, latent),
        P(LAYER, None, latent, None),
        P(LAYER, latent),
    )
    out_specs = (
        P(LAYER, None, latent, TOK),
        P(LAYER, latent),
        P(LAYER, TOK, latent),
        P(LAYER, latent),
    )
    return jax.shard_map(
        on_device, mesh=fine, in_specs=in_specs, out_specs=out_specs, check_vma=False
    )
```

```python
import functools
import math

import jax
import jax.numpy as jnp
from jax import lax
from jax.experimental import pallas as pl
from jax.experimental.pallas import tpu as pltpu
from jax.sharding import PartitionSpec as P

LAYER, LX, LZ, TOK = "layer", "lx", "lz", "tok"
BF16, F32 = jnp.bfloat16, jnp.float32
VMEM_MIB, LARGE_MIB = 28, 56


def smooth(values):
    return jax.nn.gelu(values, approximate=True)


def shift(value, axis, step):
    n = lax.axis_size(axis)
    return lax.ppermute(value, axis, [(i, (i + step) % n) for i in range(n)])


def send_up(value, step):
    n = lax.axis_size(LAYER)
    pairs = [(i, i + step) for i in range(n) if 0 <= i + step < n]
    return lax.ppermute(value, LAYER, pairs)


def swap(value):
    return lax.ppermute(value, TOK, [(0, 1), (1, 0)])


def turned(value, axis, by):
    n = value.shape[axis]
    return lax.dynamic_slice_in_dim(jnp.concatenate([value, value], axis), by, n, axis)


def total(values):
    return functools.reduce(jnp.add, [v.astype(F32) for v in values])


def spread(value, axis):
    return [value[0]] + [shift(value[k], axis, k) for k in range(1, len(value))]


def gathered(value, axis):
    n = lax.axis_size(axis)
    return [value] + [shift(value, axis, -k) for k in range(1, n)]


def call(kernel, where, inputs, in_specs, outs, out_specs, grid, scratch, flops, moved, aliases=None, mib=VMEM_MIB):
    return pl.pallas_call(
        kernel,
        out_shape=[jax.ShapeDtypeStruct(shape, dtype) for shape, dtype in outs],
        grid_spec=pltpu.PrefetchScalarGridSpec(
            num_scalar_prefetch=1,
            grid=(grid,),
            in_specs=in_specs,
            out_specs=out_specs,
            scratch_shapes=scratch,
        ),
        input_output_aliases=aliases or {},
        compiler_params=pltpu.CompilerParams(vmem_limit_bytes=mib * 2**20),
        cost_estimate=pl.CostEstimate(flops=flops, bytes_accessed=moved, transcendentals=0),
    )(where, *inputs)


def fixed(*shape):
    return pl.BlockSpec(shape, lambda k, w: (0,) * len(shape))


def each(*shape):
    return pl.BlockSpec(shape, lambda k, w: (k,) + (0,) * (len(shape) - 1))


def encode_kernel(where, in_ref, w_ref, bias_ref, pre_ref, lat_ref, turned_ref, acc_ref, *, ring):
    k = pl.program_id(0)

    @pl.when(k == 0)
    def _():
        acc_ref[...] = jnp.broadcast_to(bias_ref[...], acc_ref.shape)

    acc_ref[...] += jnp.dot(in_ref[...], w_ref[...], preferred_element_type=F32)

    @pl.when(k == pl.num_programs(0) - 1)
    def _():
        piece = acc_ref.shape[0] // (ring * ring)
        for i in range(ring):
            for j in range(ring):
                row, col = lax.rem(i + ring - where[2], ring), lax.rem(j + ring - where[3], ring)
                pre = acc_ref[(i * ring + j) * piece : (i * ring + j + 1) * piece, :]
                latent = smooth(pre).astype(BF16)
                to = pl.ds(pl.multiple_of((row * ring + col) * piece, piece), piece)
                pre_ref[to, :] = pre
                lat_ref[to, :] = latent
                turned_ref[pl.ds(pl.multiple_of((col * ring + row) * piece, piece), piece), :] = latent


def encode(where, inputs, weight, bias, ring, steps=3):
    rows, model = inputs.shape
    feats = weight.shape[1]
    return call(
        functools.partial(encode_kernel, ring=ring),
        where,
        (inputs, weight, bias),
        [
            pl.BlockSpec((rows, model // steps), lambda k, w: (0, k)),
            pl.BlockSpec((model // steps, feats), lambda k, w: (k, 0)),
            fixed(1, feats),
        ],
        [((rows, feats), F32), ((rows, feats), BF16), ((rows, feats), BF16)],
        [fixed(rows, feats)] * 3,
        steps,
        [pltpu.VMEM((rows, feats), F32)],
        2 * rows * model * feats,
        8 * 2**20,
        mib=LARGE_MIB,
    )


def far_kernel(where, own_ref, other_ref, w_ref, *out_refs):
    for lat_ref, refs in ((own_ref, out_refs[:2]), (other_ref, out_refs[2:])):
        n = lat_ref.shape[0] // 4
        out = jnp.dot(lat_ref[2 * n : 3 * n, :], w_ref[0], preferred_element_type=F32).astype(BF16)
        refs[0][0] = out[: n // 2]
        refs[1][0] = out[n // 2 :]


def near_kernel(where, own_ref, other_ref, w_ref, *out_refs):
    for lat_ref, refs in ((own_ref, out_refs[:3]), (other_ref, out_refs[3:])):
        n = lat_ref.shape[0] // 4
        out = jnp.dot(lat_ref[: 2 * n, :], w_ref[0], preferred_element_type=F32)
        refs[0][0] = out[:n]
        refs[1][0] = out[n:].astype(BF16)
        out = jnp.dot(lat_ref[3 * n :, :], w_ref[0], preferred_element_type=F32)
        refs[2][0] = out.astype(BF16)


def rebuild(kernel, where, own_lat, other_lat, weights, width):
    layers, feats, _ = weights.shape
    rows = own_lat.shape[0]
    n = rows // 4
    half = ((layers, n // 2, width), BF16)
    if kernel is far_kernel:
        outs, used = [half] * 4, 2 * n
    else:
        outs, used = [((layers, n, width), d) for d in (F32, BF16, BF16)] * 2, 6 * n
    return call(
        kernel,
        where,
        (own_lat, other_lat, weights),
        [
            fixed(rows, feats),
            fixed(rows, feats),
            pl.BlockSpec((1, feats, width), lambda k, w: (lax.rem(w[0] + k, layers), 0, 0)),
        ],
        outs,
        [each(1, *shape[1:]) for shape, _ in outs],
        layers,
        [],
        2 * layers * used * feats * width,
        8 * 2**20,
        mib=VMEM_MIB if kernel is far_kernel else LARGE_MIB,
    )


def fold_kernel(where, *refs):
    for i in range(4):
        value, rows, out = refs[i], refs[4 + i], refs[8 + i]
        out[...] = (value[...].astype(F32) + rows[...].astype(F32)).astype(BF16)


def fold(where, values, rows, steps=2):
    layers, n, width = values[0].shape
    half = (layers // steps, n // 2, width)
    low, high = pl.BlockSpec(half, lambda k, w: (k, 0, 0)), pl.BlockSpec(half, lambda k, w: (k, 1, 0))
    return call(
        fold_kernel,
        where,
        (*values, *rows),
        [low, high, low, high] + [each(*half)] * 4,
        [(v.shape, BF16) for v in values],
        [low, high, low, high],
        steps,
        [],
        4 * values[0].size,
        12 * values[0].size,
        {1 + i: i for i in range(4)},
    )


def near_act_kernel(where, w_ref, *refs):
    *x_refs, act_ref, err_ref = refs
    k = pl.program_id(0)
    step = x_refs[0].shape[1]

    @pl.when(k == 0)
    def _():
        act_ref[...] = jnp.zeros_like(act_ref)

    @pl.when(where[0] + k < pl.num_programs(0))
    def _():
        for i, x_ref in enumerate(x_refs):
            err_ref[i * step : (i + 1) * step, :] = x_ref[0]
        for i in range(0, err_ref.shape[0], 256):
            act_ref[i : i + 256, :] += lax.dot_general(
                err_ref[i : i + 256, :], w_ref[0], (((1,), (1,)), ((), ())), preferred_element_type=F32
            )


def far_act_kernel(where, w_ref, near_ref, *refs, ring):
    *x_refs, own_ref, other_ref, err_ref, act_ref = refs
    k = pl.program_id(0)
    step = x_refs[0].shape[1]

    @pl.when(k == 0)
    def _():
        act_ref[...] = jnp.zeros_like(act_ref)

    @pl.when(where[0] + k < pl.num_programs(0))
    def _():
        for i, x_ref in enumerate(x_refs):
            err_ref[i * step : (i + 1) * step, :] = x_ref[0]
        act_ref[...] += lax.dot_general(
            err_ref[...], w_ref[0], (((1,), (1,)), ((), ())), preferred_element_type=F32
        )

    @pl.when(k == pl.num_programs(0) - 1)
    def _():
        n = act_ref.shape[0] // 2
        piece = n // ring
        for side in range(2):
            for i in range(ring):
                ref, at = {
                    0: (near_ref, 3 * n * side),
                    1: (near_ref, 3 * n * side + n),
                    2: (act_ref, n * side),
                    3: (near_ref, 3 * n * side + 2 * n),
                }[i]
                if side == 0:
                    own_ref[i * n : (i + 1) * n, :] = ref[at : at + n, :]
                else:
                    for j in range(ring):
                        to = (j * ring + i) * piece
                        other_ref[to : to + piece, :] = ref[at + j * piece : at + (j + 1) * piece, :]


def act_grads(where, weights, near, far, width, ring):
    layers, feats, _ = weights.shape
    n = near[0].shape[1]
    target = pl.BlockSpec((1, feats, width), lambda k, w: (lax.rem(w[0] + k, layers), 0, 0))
    [act] = call(
        near_act_kernel,
        where,
        (weights, *near),
        [target] + [each(1, n, width)] * 6,
        [((6 * n, feats), F32)],
        [fixed(6 * n, feats)],
        layers,
        [pltpu.VMEM((6 * n, width), BF16)],
        2 * layers * 6 * n * feats * width,
        14 * 2**20,
    )
    return call(
        functools.partial(far_act_kernel, ring=ring),
        where,
        (weights, act, *far),
        [target, fixed(6 * n, feats)] + [each(1, n // 2, width)] * 4,
        [((4 * n, feats), F32)] * 2,
        [fixed(4 * n, feats)] * 2,
        layers,
        [pltpu.VMEM((2 * n, width), BF16), pltpu.VMEM((2 * n, feats), F32)],
        2 * layers * 2 * n * feats * width,
        10 * 2**20,
    )


def dec_kernel(where, own_ref, other_ref, *refs):
    *x_refs, dec_ref, sum_ref, err_ref = refs
    live = where[0] + pl.program_id(0) < pl.num_programs(0)
    rows = own_ref.shape[0]

    @pl.when(live)
    def _():
        half = x_refs[-1].shape[1]
        starts = [0, 2, 6, 8, 10, 14, 4, 5, 12, 13]
        for x_ref, start in zip(x_refs, starts, strict=True):
            err_ref[start * half : start * half + x_ref.shape[1], :] = x_ref[0]
        dims = (((0,), (0,)), ((), ()))
        dec_ref[0] = lax.dot_general(
            own_ref[...], err_ref[:rows, :], dims, preferred_element_type=F32
        ) + lax.dot_general(other_ref[...], err_ref[rows:, :], dims, preferred_element_type=F32)

    @pl.when(jnp.logical_not(live))
    def _():
        dec_ref[0] = jnp.zeros_like(dec_ref[0])

    @pl.when(pl.program_id(0) == 0)
    def _():
        sum_ref[...] = jnp.sum(err_ref[...].astype(F32), axis=0, keepdims=True)


def dec_gradient(where, own_lat, other_lat, errs):
    rows, feats = own_lat.shape
    layers, _, width = errs[0].shape
    return call(
        dec_kernel,
        where,
        (own_lat, other_lat, *errs),
        [fixed(rows, feats)] * 2 + [each(1, e.shape[1], width) for e in errs],
        [((layers, feats, width), F32), ((1, width), F32)],
        [
            pl.BlockSpec((1, feats, width), lambda k, w: (lax.rem(w[0] + k, layers), 0, 0)),
            fixed(1, width),
        ],
        layers,
        [pltpu.VMEM((2 * rows, width), BF16)],
        4 * layers * rows * feats * width,
        20 * 2**20,
    )


def enc_kernel(where, in_ref, other_ref, grad_ref, other_grad_ref, out_ref):
    out_ref[...] = jnp.dot(in_ref[...], grad_ref[...], preferred_element_type=F32) + jnp.dot(
        other_ref[...], other_grad_ref[...], preferred_element_type=F32
    )


def enc_gradient(where, own_t, other_t, grad, other_grad, steps=6):
    width, rows = own_t.shape
    feats = grad.shape[1]
    tile = pl.BlockSpec((width // steps, rows), lambda k, w: (k, 0))
    return call(
        enc_kernel,
        where,
        (own_t, other_t, grad, other_grad),
        [tile, tile, fixed(rows, feats), fixed(rows, feats)],
        [((width, feats), F32)],
        [pl.BlockSpec((width // steps, feats), lambda k, w: (k, 0))],
        steps,
        [],
        4 * rows * width * feats,
        6 * 2**20,
    )[0]


def on_device(resid_in, resid_out, enc_weight, enc_bias, dec_weight, dec_bias):
    s, x, z, c = (lax.axis_index(a) for a in (LAYER, LX, LZ, TOK))
    ring = lax.axis_size(LX)
    layers, feats, model = dec_weight.shape[1:]
    tok = resid_in.shape[1]
    width = model // 2
    piece = tok // (ring * ring)
    scale = 1.0 / math.sqrt(tok * lax.axis_size(TOK))
    where = jnp.stack([s, c, x, z]).astype(jnp.int32)
    inputs = resid_in[0]
    weights = lax.dynamic_slice_in_dim(dec_weight[0], c * width, width, 2)

    def mine_first(rows):
        blocks = rows.reshape(ring, ring, piece, rows.shape[1])
        return turned(turned(blocks, 0, x), 1, z).reshape(rows.shape)

    pre, own_lat, crossed = encode(where, inputs, enc_weight[0], enc_bias, ring)
    other_lat = swap(crossed)

    far_a0, far_a1, far_b0, far_b1 = rebuild(far_kernel, where, own_lat, other_lat, weights, width)
    parts = [(far_a0, LX, 1), (far_a1, LX, -1), (far_b0, LZ, 1), (far_b1, LZ, -1)]
    got = [shift(*part) for part in parts]
    own_a, up_a, down_a, own_b, up_b, down_b = rebuild(
        near_kernel, where, own_lat, other_lat, weights, width
    )
    out_in, own_a = lax.optimization_barrier((resid_out[0], own_a))
    base = dec_bias[0] - out_in.astype(F32).reshape(ring * ring, piece, -1)
    base = lax.all_to_all(base, (LX, LZ), 0, 0, tiled=True)
    folded = fold(where, (up_a, down_a, up_b, down_b), got)
    got = [shift(value, *part[1:]) for value, part in zip(folded, parts, strict=True)]

    later, *_ = lax.optimization_barrier((inputs, *folded))
    ordered = mine_first(later)
    own_in = lax.dynamic_slice_in_dim(ordered, c * width, width, 1)
    to_other = lax.dynamic_slice_in_dim(ordered, (1 - c) * width, width, 1)
    own_in = own_in.T

    base, own_in, to_other = lax.optimization_barrier((base, own_in, to_other))
    halves = base.reshape(2, ring * ring // 2, piece, -1)
    own_base, other_base = (
        lax.dynamic_index_in_dim(halves, core, 0, False).transpose(1, 0, 2).reshape(piece, width)
        for core in (c, 1 - c)
    )
    base = jnp.stack([own_base, swap(other_base)])

    def settled(own, below, above):
        cuts = [slice(i * piece, (i + 1) * piece) for i in range(ring)]
        sums = [total([v[:, cut] for v in (own, below, above)]) for cut in cuts]
        return [sums[0]] + [v.astype(BF16) for v in sums[1:]]

    a = spread(settled(own_a, *got[:2]), LZ)
    b = spread(settled(own_b, *got[2:]), LX)
    base, b[3] = lax.optimization_barrier((base, b[3]))
    a, b = total(a), total(b)
    pieces = jnp.stack([a, b], 1)
    rebuilt = pieces[0] + base
    for k in range(1, layers):
        rebuilt = rebuilt + send_up(pieces[k].astype(BF16), k).astype(F32)
    errors = (rebuilt * scale).astype(BF16)

    errors, to_other = lax.optimization_barrier((errors, to_other))
    other_in = swap(to_other).T
    errors = jnp.stack([errors] + [send_up(errors, -k) for k in range(1, layers)], 1)
    paths = [(LX, -1), (LX, 1), (LZ, -1), (LZ, 1)]
    own_a = jnp.concatenate(gathered(errors[0], LZ), 1)
    own_b = jnp.concatenate(gathered(errors[1], LX), 1)
    got = [shift(v, *path) for v, path in zip((own_a, own_a, own_b, own_b), paths, strict=True)]
    half = got[0].shape[1] // 2
    far = [
        shift(v[:, i % 2 * half : (i % 2 + 1) * half], *path)
        for i, (v, path) in enumerate(zip(got, paths, strict=True))
    ]
    own_in, other_in, *got = lax.optimization_barrier((own_in, other_in, *got))
    near = [own_a, *got[:2], own_b, *got[2:]]

    own_act, other_act = act_grads(where, weights, near, far, width, ring)
    dec_grad, sums = dec_gradient(where, own_lat, other_lat, [*near, *far])
    pre, sums = lax.optimization_barrier((pre, sums))
    act = own_act + swap(other_act)
    pre_grad = jax.vjp(smooth, pre)[1](act)[0].astype(BF16)
    own_sum = jnp.sum(pre_grad.astype(F32), axis=0, keepdims=True)
    enc_grad = enc_gradient(where, own_in, other_in, pre_grad, swap(pre_grad))
    enc_bias_grad = own_sum + swap(own_sum)
    both = turned(jnp.concatenate([sums, swap(sums)], 0), 0, c).reshape(1, model)
    size = dec_bias.shape[1]
    dec_bias_grad = lax.dynamic_slice_in_dim(both, (x * ring + z) * size, size, 1)
    return dec_grad[None], dec_bias_grad, enc_grad[None], enc_bias_grad


def solution(mesh):
    ring = math.isqrt(mesh.shape["latent"])
    shape = (mesh.shape["layer"], ring, ring, mesh.shape["tok"])
    fine = jax.sharding.Mesh(mesh.devices.reshape(shape), (LAYER, LX, LZ, TOK))
    latent = (LX, LZ)
    in_specs = (
        P(LAYER, TOK, None),
        P(LAYER, TOK, latent),
        P(LAYER, None, latent),
        P(LAYER, latent),
        P(LAYER, None, latent, None),
        P(LAYER, latent),
    )
    out_specs = (
        P(LAYER, None, latent, TOK),
        P(LAYER, latent),
        P(LAYER, TOK, latent),
        P(LAYER, latent),
    )
    return jax.shard_map(
        on_device, mesh=fine, in_specs=in_specs, out_specs=out_specs, check_vma=False
    )
```

```python
import functools
import math

import jax
import jax.numpy as jnp
from jax import lax
from jax.experimental import pallas as pl
from jax.experimental.pallas import tpu as pltpu
from jax.sharding import PartitionSpec as P

LAYER, LX, LZ, TOK = "layer", "lx", "lz", "tok"
BF16, F32 = jnp.bfloat16, jnp.float32
VMEM_MIB, LARGE_MIB = 28, 56


def smooth(values):
    return jax.nn.gelu(values, approximate=True)


def shift(value, axis, step):
    n = lax.axis_size(axis)
    return lax.ppermute(value, axis, [(i, (i + step) % n) for i in range(n)])


def send_up(value, step):
    n = lax.axis_size(LAYER)
    pairs = [(i, i + step) for i in range(n) if 0 <= i + step < n]
    return lax.ppermute(value, LAYER, pairs)


def swap(value):
    return lax.ppermute(value, TOK, [(0, 1), (1, 0)])


def turned(value, axis, by):
    n = value.shape[axis]
    return lax.dynamic_slice_in_dim(jnp.concatenate([value, value], axis), by, n, axis)


def total(values):
    return functools.reduce(jnp.add, [v.astype(F32) for v in values])


def spread(value, axis):
    return [value[0]] + [shift(value[k], axis, k) for k in range(1, len(value))]


def gathered(value, axis):
    n = lax.axis_size(axis)
    return [value] + [shift(value, axis, -k) for k in range(1, n)]


def call(kernel, where, inputs, in_specs, outs, out_specs, grid, scratch, flops, moved, aliases=None, mib=VMEM_MIB):
    return pl.pallas_call(
        kernel,
        out_shape=[jax.ShapeDtypeStruct(shape, dtype) for shape, dtype in outs],
        grid_spec=pltpu.PrefetchScalarGridSpec(
            num_scalar_prefetch=1,
            grid=(grid,),
            in_specs=in_specs,
            out_specs=out_specs,
            scratch_shapes=scratch,
        ),
        input_output_aliases=aliases or {},
        compiler_params=pltpu.CompilerParams(vmem_limit_bytes=mib * 2**20),
        cost_estimate=pl.CostEstimate(flops=flops, bytes_accessed=moved, transcendentals=0),
    )(where, *inputs)


def fixed(*shape):
    return pl.BlockSpec(shape, lambda k, w: (0,) * len(shape))


def each(*shape):
    return pl.BlockSpec(shape, lambda k, w: (k,) + (0,) * (len(shape) - 1))


def encode_kernel(where, in_ref, w_ref, bias_ref, pre_ref, lat_ref, turned_ref, acc_ref, *, ring):
    k = pl.program_id(0)

    @pl.when(k == 0)
    def _():
        acc_ref[...] = jnp.broadcast_to(bias_ref[...], acc_ref.shape)

    acc_ref[...] += jnp.dot(in_ref[...], w_ref[...], preferred_element_type=F32)

    @pl.when(k == pl.num_programs(0) - 1)
    def _():
        piece = acc_ref.shape[0] // (ring * ring)
        for i in range(ring):
            for j in range(ring):
                row, col = lax.rem(i + ring - where[2], ring), lax.rem(j + ring - where[3], ring)
                pre = acc_ref[(i * ring + j) * piece : (i * ring + j + 1) * piece, :]
                latent = smooth(pre).astype(BF16)
                to = pl.ds(pl.multiple_of((row * ring + col) * piece, piece), piece)
                pre_ref[to, :] = pre
                lat_ref[to, :] = latent
                turned_ref[pl.ds(pl.multiple_of((col * ring + row) * piece, piece), piece), :] = latent


def encode(where, inputs, weight, bias, ring, steps=3):
    rows, model = inputs.shape
    feats = weight.shape[1]
    return call(
        functools.partial(encode_kernel, ring=ring),
        where,
        (inputs, weight, bias),
        [
            pl.BlockSpec((rows, model // steps), lambda k, w: (0, k)),
            pl.BlockSpec((model // steps, feats), lambda k, w: (k, 0)),
            fixed(1, feats),
        ],
        [((rows, feats), F32), ((rows, feats), BF16), ((rows, feats), BF16)],
        [fixed(rows, feats)] * 3,
        steps,
        [pltpu.VMEM((rows, feats), F32)],
        2 * rows * model * feats,
        8 * 2**20,
        mib=LARGE_MIB,
    )


def far_kernel(where, own_ref, other_ref, w_ref, *out_refs):
    for lat_ref, refs in ((own_ref, out_refs[:2]), (other_ref, out_refs[2:])):
        n = lat_ref.shape[0] // 4
        out = jnp.dot(lat_ref[2 * n : 3 * n, :], w_ref[0], preferred_element_type=F32).astype(BF16)
        refs[0][0] = out[: n // 2]
        refs[1][0] = out[n // 2 :]


def near_kernel(where, own_ref, other_ref, w_ref, *out_refs):
    for lat_ref, refs in ((own_ref, out_refs[:3]), (other_ref, out_refs[3:])):
        n = lat_ref.shape[0] // 4
        out = jnp.dot(lat_ref[: 2 * n, :], w_ref[0], preferred_element_type=F32)
        refs[0][0] = out[:n]
        refs[1][0] = out[n:].astype(BF16)
        out = jnp.dot(lat_ref[3 * n :, :], w_ref[0], preferred_element_type=F32)
        refs[2][0] = out.astype(BF16)


def rebuild(kernel, where, own_lat, other_lat, weights, width):
    layers, feats, _ = weights.shape
    rows = own_lat.shape[0]
    n = rows // 4
    half = ((layers, n // 2, width), BF16)
    if kernel is far_kernel:
        outs, used = [half] * 4, 2 * n
    else:
        outs, used = [((layers, n, width), d) for d in (F32, BF16, BF16)] * 2, 6 * n
    return call(
        kernel,
        where,
        (own_lat, other_lat, weights),
        [
            fixed(rows, feats),
            fixed(rows, feats),
            pl.BlockSpec((1, feats, width), lambda k, w: (lax.rem(w[0] + k, layers), 0, 0)),
        ],
        outs,
        [each(1, *shape[1:]) for shape, _ in outs],
        layers,
        [],
        2 * layers * used * feats * width,
        8 * 2**20,
        mib=VMEM_MIB if kernel is far_kernel else LARGE_MIB,
    )


def fold_kernel(where, *refs):
    for i in range(4):
        value, rows, out = refs[i], refs[4 + i], refs[8 + i]
        out[...] = (value[...].astype(F32) + rows[...].astype(F32)).astype(BF16)


def fold(where, values, rows, steps=2):
    layers, n, width = values[0].shape
    half = (layers // steps, n // 2, width)
    low, high = pl.BlockSpec(half, lambda k, w: (k, 0, 0)), pl.BlockSpec(half, lambda k, w: (k, 1, 0))
    return call(
        fold_kernel,
        where,
        (*values, *rows),
        [low, high, low, high] + [each(*half)] * 4,
        [(v.shape, BF16) for v in values],
        [low, high, low, high],
        steps,
        [],
        4 * values[0].size,
        12 * values[0].size,
        {1 + i: i for i in range(4)},
    )


def near_act_kernel(where, w_ref, *refs):
    *x_refs, act_ref, sum_ref, err_ref = refs
    k = pl.program_id(0)
    step = x_refs[0].shape[1]

    @pl.when(k == 0)
    def _():
        act_ref[...] = jnp.zeros_like(act_ref)

    @pl.when(where[0] + k < pl.num_programs(0))
    def _():
        for i, x_ref in enumerate(x_refs):
            err_ref[i * step : (i + 1) * step, :] = x_ref[0]
        for i in range(0, err_ref.shape[0], 256):
            act_ref[i : i + 256, :] += lax.dot_general(
                err_ref[i : i + 256, :], w_ref[0], (((1,), (1,)), ((), ())), preferred_element_type=F32
            )

    @pl.when(k == 0)
    def _():
        sum_ref[...] = jnp.sum(err_ref[...].astype(F32), axis=0, keepdims=True)


def far_act_kernel(where, w_ref, near_ref, near_sum_ref, *refs, ring):
    *x_refs, own_ref, other_ref, sum_ref, err_ref, act_ref = refs
    k = pl.program_id(0)
    step = x_refs[0].shape[1]

    @pl.when(k == 0)
    def _():
        act_ref[...] = jnp.zeros_like(act_ref)

    @pl.when(where[0] + k < pl.num_programs(0))
    def _():
        for i, x_ref in enumerate(x_refs):
            err_ref[i * step : (i + 1) * step, :] = x_ref[0]
        act_ref[...] += lax.dot_general(
            err_ref[...], w_ref[0], (((1,), (1,)), ((), ())), preferred_element_type=F32
        )

    @pl.when(k == 0)
    def _():
        sum_ref[...] = near_sum_ref[...] + jnp.sum(err_ref[...].astype(F32), axis=0, keepdims=True)

    @pl.when(k == pl.num_programs(0) - 1)
    def _():
        n = act_ref.shape[0] // 2
        piece = n // ring
        for side in range(2):
            for i in range(ring):
                ref, at = {
                    0: (near_ref, 3 * n * side),
                    1: (near_ref, 3 * n * side + n),
                    2: (act_ref, n * side),
                    3: (near_ref, 3 * n * side + 2 * n),
                }[i]
                if side == 0:
                    own_ref[i * n : (i + 1) * n, :] = ref[at : at + n, :]
                else:
                    for j in range(ring):
                        to = (j * ring + i) * piece
                        other_ref[to : to + piece, :] = ref[at + j * piece : at + (j + 1) * piece, :]


def act_grads(where, weights, near, far, width, ring):
    layers, feats, _ = weights.shape
    n = near[0].shape[1]
    target = pl.BlockSpec((1, feats, width), lambda k, w: (lax.rem(w[0] + k, layers), 0, 0))
    act, sums = call(
        near_act_kernel,
        where,
        (weights, *near),
        [target] + [each(1, n, width)] * 6,
        [((6 * n, feats), F32), ((1, width), F32)],
        [fixed(6 * n, feats), fixed(1, width)],
        layers,
        [pltpu.VMEM((6 * n, width), BF16)],
        2 * layers * 6 * n * feats * width,
        14 * 2**20,
    )
    return call(
        functools.partial(far_act_kernel, ring=ring),
        where,
        (weights, act, sums, *far),
        [target, fixed(6 * n, feats), fixed(1, width)] + [each(1, n // 2, width)] * 4,
        [((4 * n, feats), F32)] * 2 + [((1, width), F32)],
        [fixed(4 * n, feats)] * 2 + [fixed(1, width)],
        layers,
        [pltpu.VMEM((2 * n, width), BF16), pltpu.VMEM((2 * n, feats), F32)],
        2 * layers * 2 * n * feats * width,
        10 * 2**20,
    )


def dec_kernel(where, own_ref, other_ref, *refs):
    *x_refs, dec_ref, mark_ref, err_ref = refs
    live = where[0] + pl.program_id(0) < pl.num_programs(0)
    rows = own_ref.shape[0]

    @pl.when(live)
    def _():
        half = x_refs[-1].shape[1]
        starts = [0, 2, 6, 8, 10, 14, 4, 5, 12, 13]
        for x_ref, start in zip(x_refs, starts, strict=True):
            err_ref[start * half : start * half + x_ref.shape[1], :] = x_ref[0]
        dims = (((0,), (0,)), ((), ()))
        dec_ref[0] = lax.dot_general(
            own_ref[...], err_ref[:rows, :], dims, preferred_element_type=F32
        ) + lax.dot_general(other_ref[...], err_ref[rows:, :], dims, preferred_element_type=F32)

    @pl.when(jnp.logical_not(live))
    def _():
        dec_ref[0] = jnp.zeros_like(dec_ref[0])

    @pl.when(pl.program_id(0) == 0)
    def _():
        mark_ref[...] = jnp.zeros_like(mark_ref)


def dec_gradient(where, own_lat, other_lat, errs):
    rows, feats = own_lat.shape
    layers, _, width = errs[0].shape
    return call(
        dec_kernel,
        where,
        (own_lat, other_lat, *errs),
        [fixed(rows, feats)] * 2 + [each(1, e.shape[1], width) for e in errs],
        [((layers, feats, width), F32), ((1, width), F32)],
        [
            pl.BlockSpec((1, feats, width), lambda k, w: (lax.rem(w[0] + k, layers), 0, 0)),
            fixed(1, width),
        ],
        layers,
        [pltpu.VMEM((2 * rows, width), BF16)],
        4 * layers * rows * feats * width,
        20 * 2**20,
    )


def enc_kernel(where, in_ref, other_ref, grad_ref, other_grad_ref, out_ref):
    out_ref[...] = jnp.dot(in_ref[...], grad_ref[...], preferred_element_type=F32) + jnp.dot(
        other_ref[...], other_grad_ref[...], preferred_element_type=F32
    )


def enc_gradient(where, own_t, other_t, grad, other_grad, steps=6):
    width, rows = own_t.shape
    feats = grad.shape[1]
    tile = pl.BlockSpec((width // steps, rows), lambda k, w: (k, 0))
    return call(
        enc_kernel,
        where,
        (own_t, other_t, grad, other_grad),
        [tile, tile, fixed(rows, feats), fixed(rows, feats)],
        [((width, feats), F32)],
        [pl.BlockSpec((width // steps, feats), lambda k, w: (k, 0))],
        steps,
        [],
        4 * rows * width * feats,
        6 * 2**20,
    )[0]


def on_device(resid_in, resid_out, enc_weight, enc_bias, dec_weight, dec_bias):
    s, x, z, c = (lax.axis_index(a) for a in (LAYER, LX, LZ, TOK))
    ring = lax.axis_size(LX)
    layers, feats, model = dec_weight.shape[1:]
    tok = resid_in.shape[1]
    width = model // 2
    piece = tok // (ring * ring)
    scale = 1.0 / math.sqrt(tok * lax.axis_size(TOK))
    where = jnp.stack([s, c, x, z]).astype(jnp.int32)
    inputs = resid_in[0]
    weights = lax.dynamic_slice_in_dim(dec_weight[0], c * width, width, 2)

    def mine_first(rows):
        blocks = rows.reshape(ring, ring, piece, rows.shape[1])
        return turned(turned(blocks, 0, x), 1, z).reshape(rows.shape)

    pre, own_lat, crossed = encode(where, inputs, enc_weight[0], enc_bias, ring)
    other_lat = swap(crossed)

    far_a0, far_a1, far_b0, far_b1 = rebuild(far_kernel, where, own_lat, other_lat, weights, width)
    parts = [(far_a0, LX, 1), (far_a1, LX, -1), (far_b0, LZ, 1), (far_b1, LZ, -1)]
    got = [shift(*part) for part in parts]
    own_a, up_a, down_a, own_b, up_b, down_b = rebuild(
        near_kernel, where, own_lat, other_lat, weights, width
    )
    out_in, own_a = lax.optimization_barrier((resid_out[0], own_a))
    base = dec_bias[0] - out_in.astype(F32).reshape(ring * ring, piece, -1)
    base = lax.all_to_all(base, (LX, LZ), 0, 0, tiled=True)
    folded = fold(where, (up_a, down_a, up_b, down_b), got)
    got = [shift(value, *part[1:]) for value, part in zip(folded, parts, strict=True)]

    later, *_ = lax.optimization_barrier((inputs, *folded))
    ordered = mine_first(later)
    own_in = lax.dynamic_slice_in_dim(ordered, c * width, width, 1)
    to_other = lax.dynamic_slice_in_dim(ordered, (1 - c) * width, width, 1)
    own_in = own_in.T

    base, own_in, to_other = lax.optimization_barrier((base, own_in, to_other))
    halves = base.reshape(2, ring * ring // 2, piece, -1)
    own_base, other_base = (
        lax.dynamic_index_in_dim(halves, core, 0, False).transpose(1, 0, 2).reshape(piece, width)
        for core in (c, 1 - c)
    )
    base = jnp.stack([own_base, swap(other_base)])

    def settled(own, below, above):
        cuts = [slice(i * piece, (i + 1) * piece) for i in range(ring)]
        sums = [total([v[:, cut] for v in (own, below, above)]) for cut in cuts]
        return [sums[0]] + [v.astype(BF16) for v in sums[1:]]

    a = spread(settled(own_a, *got[:2]), LZ)
    b = spread(settled(own_b, *got[2:]), LX)
    base, b[3] = lax.optimization_barrier((base, b[3]))
    a, b = total(a), total(b)
    pieces = jnp.stack([a, b], 1)
    rebuilt = pieces[0] + base
    for k in range(1, layers):
        rebuilt = rebuilt + send_up(pieces[k].astype(BF16), k).astype(F32)
    errors = (rebuilt * scale).astype(BF16)

    errors, to_other = lax.optimization_barrier((errors, to_other))
    other_in = swap(to_other).T
    errors = jnp.stack([errors] + [send_up(errors, -k) for k in range(1, layers)], 1)
    paths = [(LX, -1), (LX, 1), (LZ, -1), (LZ, 1)]
    own_a = jnp.concatenate(gathered(errors[0], LZ), 1)
    own_b = jnp.concatenate(gathered(errors[1], LX), 1)
    got = [shift(v, *path) for v, path in zip((own_a, own_a, own_b, own_b), paths, strict=True)]
    half = got[0].shape[1] // 2
    far = [
        shift(v[:, i % 2 * half : (i % 2 + 1) * half], *path)
        for i, (v, path) in enumerate(zip(got, paths, strict=True))
    ]
    own_in, other_in, *got = lax.optimization_barrier((own_in, other_in, *got))
    near = [own_a, *got[:2], own_b, *got[2:]]

    own_act, other_act, sums = act_grads(where, weights, near, far, width, ring)
    dec_grad, mark = dec_gradient(where, own_lat, other_lat, [*near, *far])
    other_sums = swap(sums)
    pre, mark, other_sums = lax.optimization_barrier((pre, mark, other_sums))
    act = own_act + swap(other_act)
    pre_grad = jax.vjp(smooth, pre)[1](act)[0].astype(BF16)
    own_sum = jnp.sum(pre_grad.astype(F32), axis=0, keepdims=True)
    enc_grad = enc_gradient(where, own_in, other_in, pre_grad, swap(pre_grad))
    enc_bias_grad = own_sum + swap(own_sum)
    both = turned(jnp.concatenate([sums, other_sums], 0), 0, c).reshape(1, model)
    size = dec_bias.shape[1]
    dec_bias_grad = lax.dynamic_slice_in_dim(both, (x * ring + z) * size, size, 1)
    return dec_grad[None], dec_bias_grad, enc_grad[None], enc_bias_grad


def solution(mesh):
    ring = math.isqrt(mesh.shape["latent"])
    shape = (mesh.shape["layer"], ring, ring, mesh.shape["tok"])
    fine = jax.sharding.Mesh(mesh.devices.reshape(shape), (LAYER, LX, LZ, TOK))
    latent = (LX, LZ)
    in_specs = (
        P(LAYER, TOK, None),
        P(LAYER, TOK, latent),
        P(LAYER, None, latent),
        P(LAYER, latent),
        P(LAYER, None, latent, None),
        P(LAYER, latent),
    )
    out_specs = (
        P(LAYER, None, latent, TOK),
        P(LAYER, latent),
        P(LAYER, TOK, latent),
        P(LAYER, latent),
    )
    return jax.shard_map(
        on_device, mesh=fine, in_specs=in_specs, out_specs=out_specs, check_vma=False
    )
```
